512 devices in a mesh: ctx: 64 (over y, z), exp: 8 (over x, core).
Axes of the slice: x: 4, y: 4, z: 16, core: 2. Of those that a mesh axis runs over, the one named last changes fastest.
Arguments:
- ssm_input: bfloat16 [8192, 4096], P('ctx', 'exp'), may hold values from -6 to 6
- gate_input: bfloat16 [8192, 4096], P('ctx', 'exp'), may hold values from -6 to 6
- b_input: bfloat16 [8192, 1024], P('ctx', 'exp'), may hold values from -6 to 6
- c_input: bfloat16 [8192, 1024], P('ctx', 'exp'), may hold values from -6 to 6
- step_size: float32 [64, 8192], P('exp', 'ctx'), may hold values from 0.5 to 16384
- decay_rate: float32 [64], P('exp'), may hold values from 2.4414063e-05 to 0.1
- norm_gain: float32 [4096], P('exp'), may hold values from 0.1 to 1.9
- out_weight: bfloat16 [4096, 2048], P('exp'), may hold values from -0.125 to 0.125
- stream: bfloat16 [8192, 2048], P('ctx', 'exp'), may hold values from -7 to 7
- moe_gain: float32 [2048], replicated, may hold values from 0.1 to 1.9
- router: bfloat16 [2048, 64], replicated, may hold values from -0.125 to 0.125
- expert_ids: int32 [8192, 6], P('ctx'), may hold values from 0 to 63, all different within a row; in each aligned block of 128 rows (0 to 127, 128 to 255, ...) at most 15 rows name the same one
- w_gate: bfloat16 [64, 1408, 2048], P('ctx', 'exp'), may hold values from -0.125 to 0.125
- w_up: bfloat16 [64, 1408, 2048], P('ctx', 'exp'), may hold values from -0.125 to 0.125
- w_down: bfloat16 [64, 1408, 2048], P('ctx', 'exp'), may hold values from -0.21875 to 0.21875
Outputs:
- layer_out: bfloat16 [8192, 2048], P('ctx', 'exp')
The draws below stay inside these ranges and needn't reach their ends.
Inputs may be any that keep to these rules, and one draw needn't show every extreme that they name: `expert_ids`: each row names 6 different experts; among the 128 rows of one device (aligned blocks of 128 rows) no expert is named by more than 15 rows, a bound that some block reaches.
All inputs are finite; a program needn't handle non-finite values.
Results may differ from the reference program's by a relative error of at most 0.024.
Values may be sent and summed in bfloat16 or wider, within the bound.
A program may use at most 64 MiB of HBM per device.

```python
import math
import jax
import jax.numpy as jnp
import numpy as np
from jax import lax

D = 2048
HEADS = 64
P_SIZE = 64
N = 128
GROUPS = 8
FF = 1408
TOP = 6
TOK_DEV = 128
TOKENS = 8192
EXPERTS = 64
CAP = 15
N_CTX = 64
N_EXP = 8


def rate_table(key):
    base_key = jax.random.fold_in(key, 101)
    key_slow, key_fast, key_pick = jax.random.split(base_key, 3)
    slow_rate = jnp.exp(jax.random.uniform(key_slow, (HEADS,), jnp.float32, math.log(0.2 / TOKENS), math.log(1.0 / TOKENS)))
    fast_rate = jnp.exp(jax.random.uniform(key_fast, (HEADS,), jnp.float32, math.log(0.02), math.log(0.1)))
    keep_share = 0.5
    chosen_slow = jax.random.uniform(key_pick, (HEADS,), jnp.float32) < keep_share
    return jnp.where(chosen_slow, slow_rate, fast_rate).astype(jnp.float32)


def draw_decay_rate(key, part):
    return rate_table(key)


def draw_step_size(key, part):
    speed_numbers = rate_table(key)
    base_key = jax.random.fold_in(key, 202)
    key_base, key_place, key_loss = jax.random.split(base_key, 3)
    layer_result_tensor = jnp.exp(jax.random.uniform(key_base, (HEADS, TOKENS), jnp.float32, math.log(0.5), math.log(2.0)))
    destination_entries = jax.random.randint(key_place, (3,), 0, TOKENS)
    dropped_portion = jax.random.uniform(key_loss, (3,), jnp.float32, 0.2, 0.3)
    matrix_position = jnp.arange(TOKENS)[None, :]
    for position_number in range(3):
        jump_forward_step = -jnp.log1p(-dropped_portion[position_number]) / speed_numbers[:, None]
        layer_result_tensor = jnp.where(matrix_position == destination_entries[position_number], jnp.maximum(layer_result_tensor, jump_forward_step), layer_result_tensor)
    return layer_result_tensor.astype(jnp.float32)


def draw_stream(key, part):
    base_key = jax.random.fold_in(key, 303)
    matrix_position = jnp.arange(D, dtype=jnp.float32)[None, :]
    column_rise = jnp.exp(math.log(3.0) * matrix_position / D)
    values = jnp.clip(jax.random.normal(base_key, (TOKENS, D), jnp.float32), -3.8, 3.8) * column_rise * 0.6
    return values.astype(jnp.bfloat16)


def with_spikes(array, stream_key, source, target, shards_of, factor):
    def block_of(axis_at):
        return (jnp.arange(array.shape[axis_at]) // (array.shape[axis_at] // shards_of)).reshape((-1,) + (1,) * (array.ndim - 1 - axis_at))

    near = jax.random.permutation(stream_key, shards_of)[block_of(target)]
    second = (block_of(target) + shards_of // 2) % shards_of
    return jnp.where((block_of(source) == near) | (block_of(source) == second), factor * array, array)


def block_scale(key, extent, shards, low, largest):
    def one(position, blocks):
        heights = jax.random.uniform(jax.random.fold_in(jax.random.fold_in(key, 6), position), (blocks,), jnp.float32, low / len(shards), largest / len(shards))
        return jnp.repeat(jnp.exp(heights), extent[position] // blocks).reshape((-1,) + (1,) * (len(extent) - position - 1))

    gain = one(*shards[0])
    for cut in shards[1:]:
        gain = gain * one(*cut)
    return gain


def shared_out(key, own, number, rows, number_of, top, reach, skew):
    ranking = jax.random.permutation(key, number_of)
    crowded, ordinary = load_shares(number_of, rows * top, reach, skew, True), load_shares(number_of, rows * top, reach, skew, False)
    places = jnp.arange(number_of)

    def named(tallies, turn):
        used = int((tallies > 0).sum())
        fixed = max(1, used // 4)
        shifted = fixed + (places - fixed + turn * (used - fixed)) % max(1, number_of - fixed)
        return jnp.zeros((number_of,), jnp.int32).at[ranking[jnp.where(places < fixed, places, shifted)]].set(jnp.asarray(tallies, jnp.int32))

    tallies = jnp.where(number % 4 == 0, named(crowded, number // 4), named(ordinary, number - number // 4 - 1))
    mixed = jax.random.permutation(jax.random.fold_in(own, 3), number_of)
    source_of, receiver = mixed[0:number_of // 2 * 2:2], mixed[1:number_of // 2 * 2:2]
    margin = jnp.minimum(tallies[source_of] - 1, reach - tallies[receiver]) // 2
    margin = jnp.where((source_of == ranking[0]) | (receiver == ranking[0]) | (tallies[receiver] == 0), 0, jnp.maximum(margin, 0))
    shifted = jax.random.randint(jax.random.fold_in(own, 4), (number_of // 2,), 0, 1 << 20) % (margin + 1)
    tallies = tallies.at[source_of].add(-shifted).at[receiver].add(shifted)
    items = jnp.searchsorted(jnp.cumsum(tallies), jnp.arange(rows * top), side="right").astype(jnp.int32)
    listing = items.reshape(top, rows).T
    listing = listing[jax.random.permutation(jax.random.fold_in(own, 1), rows)]
    turn = jax.random.randint(jax.random.fold_in(own, 2), (rows, 1), 0, top)
    return jnp.take_along_axis(listing, (jnp.arange(top)[None, :] + turn) % top, axis=1)


def load_shares(number_of, total, reach, lean, full):
    portions = [(1 << 20) // math.isqrt(grade ** lean) + 1 for grade in range(1, number_of + 1)]
    largest = reach if full else min(reach, max(-(-total // number_of), total * portions[0] // sum(portions)))
    least = 1 if total - largest >= number_of - 1 else 0
    counts, surplus = [largest] + [least] * (number_of - 1), total - largest - least * (number_of - 1)
    while surplus > 0:
        movable = [i for i in range(1, number_of) if counts[i] < largest] or [i for i in range(1, number_of) if counts[i] < reach]
        pool, left = sum([portions[i] for i in movable]), surplus
        for i in movable:
            more = min(reach - counts[i], max(1, left * portions[i] // pool), surplus)
            counts[i] = counts[i] + more
            surplus = surplus - more
    return np.array(counts)


def scatter_about(key, extent, scale, most, cuts=(), kind=jnp.bfloat16):
    values = jax.random.normal(key, extent, jnp.float32) * scale
    if len(cuts) > 0:
        values = block_scale(key, extent, cuts, -0.22, 0.18) * values
    return jnp.clip(values, min=-most, max=most).astype(kind)


def gaussian_with(own_key, dims, deviation, bound, cuts, heavy, kind=jnp.bfloat16):
    entries = deviation * jax.random.normal(own_key, dims, jnp.float32)
    if cuts:
        entries = entries * block_scale(own_key, dims, cuts, -0.22, 0.18)
    return jnp.clip(with_spikes(entries, jax.random.fold_in(own_key, 3), *heavy), -bound, bound).astype(kind)


def setup_inputs(seed: int = 0) -> dict:
    seeds = jax.random.split(jax.random.key(seed), 16)
    ssm_input = scatter_about(seeds[0], (TOKENS, HEADS * P_SIZE), 1.0, 6.0, ((0, 64), (1, 8)))
    gate_input = scatter_about(seeds[1], (TOKENS, HEADS * P_SIZE), 1.0, 6.0, ((0, 64), (1, 8)))
    b_input = scatter_about(seeds[2], (TOKENS, GROUPS * N), 1.0, 6.0, ((0, 64), (1, 8)))
    c_input = scatter_about(seeds[3], (TOKENS, GROUPS * N), 1.0, 6.0, ((0, 64), (1, 8)))
    step_size = draw_step_size(jax.random.fold_in(seeds[15], 71), 0)
    decay_rate = draw_decay_rate(jax.random.fold_in(seeds[15], 71), 0)
    norm_gain = jnp.clip(1.0 + 0.18 * jax.random.normal(seeds[6], (HEADS * P_SIZE,), jnp.float32), 0.1, 1.9)
    out_weight = gaussian_with(seeds[7], (HEADS * P_SIZE, D), (HEADS * P_SIZE) ** -0.5, 0.125, ((0, 8),), (0, 1, 8, 2.0))
    stream = draw_stream(jax.random.fold_in(seeds[15], 71), 0)
    moe_gain = jnp.clip(1.0 + 0.18 * jax.random.normal(seeds[9], (D,), jnp.float32), 0.1, 1.9)
    router = scatter_about(seeds[10], (D, EXPERTS), D ** -0.5, 0.125)
    expert_ids_keys = jax.random.split(jax.random.fold_in(seeds[11], 1), TOKENS // TOK_DEV)
    expert_ids_turns = jax.random.permutation(jax.random.fold_in(seeds[11], 3), TOKENS // TOK_DEV)
    expert_ids = jax.vmap(lambda own, number: shared_out(jax.random.fold_in(seeds[11], 2), own, number, TOK_DEV, EXPERTS, TOP, CAP, 2))(expert_ids_keys, expert_ids_turns).reshape((TOKENS, TOP))
    w_gate = scatter_about(seeds[12], (EXPERTS, FF, D), D ** -0.5, 0.125, ((0, 64), (1, 8)))
    w_up = scatter_about(seeds[13], (EXPERTS, FF, D), D ** -0.5, 0.125, ((0, 64), (1, 8)))
    w_down = gaussian_with(seeds[14], (EXPERTS, FF, D), FF ** -0.5, 0.21875, ((0, 64), (1, 8)), (1, 2, 8, 2.0))
    return dict(ssm_input=ssm_input, gate_input=gate_input, b_input=b_input, c_input=c_input, step_size=step_size, decay_rate=decay_rate, norm_gain=norm_gain, out_weight=out_weight, stream=stream, moe_gain=moe_gain, router=router, expert_ids=expert_ids, w_gate=w_gate, w_up=w_up, w_down=w_down)


def ssd_block(operands):
    weighted, running, b_block, c_block = operands
    scores = jnp.einsum('tgn,sgn->gts', c_block.astype(jnp.float32), b_block.astype(jnp.float32))
    ordered = running.transpose(1, 2, 0)
    spread = ordered[:, :, :, None] - ordered[:, :, None, :]
    block_len = weighted.shape[0]
    lower_mask = jnp.arange(block_len)[:, None] >= jnp.arange(block_len)[None, :]
    decay_mat = jnp.where(lower_mask, jnp.exp(jnp.where(lower_mask, spread, 0.0)), 0.0)
    mixing = (decay_mat * scores[:, None]).astype(jnp.bfloat16)
    inner = jnp.einsum('gqts,sgqp->tgqp', mixing.astype(jnp.float32), weighted.astype(jnp.float32))
    tail_decay = jnp.exp(running[-1:] - running)
    carried = (tail_decay[..., None] * weighted).astype(jnp.bfloat16)
    block_state = jnp.einsum('tgqp,tgn->gqpn', carried.astype(jnp.float32), b_block.astype(jnp.float32))
    return (inner, block_state, jnp.exp(running[-1]))

def reference(ssm_input, gate_input, b_input, c_input, step_size, decay_rate, norm_gain, out_weight, stream, moe_gain, router, expert_ids, w_gate, w_up, w_down):
    group_heads = HEADS // GROUPS
    shaped_x = ssm_input.reshape(N_CTX, TOK_DEV, GROUPS, group_heads, P_SIZE)
    step_blocks = step_size.T.reshape(N_CTX, TOK_DEV, GROUPS, group_heads)
    weighted = (step_blocks[..., None] * shaped_x).astype(jnp.bfloat16)
    log_decay = (-step_size * decay_rate[:, None]).T.reshape(N_CTX, TOK_DEV, GROUPS, group_heads)
    running = jnp.cumsum(log_decay, axis=1)
    b_blocks = b_input.reshape(N_CTX, TOK_DEV, GROUPS, N)
    c_blocks = c_input.reshape(N_CTX, TOK_DEV, GROUPS, N)
    inner, states, block_decay = lax.map(ssd_block, (weighted, running, b_blocks, c_blocks))

    def chain_step(carry, operands):
        state_now, decay_now = operands
        return (decay_now[:, :, None, None] * carry + state_now, carry)
    final_state, entering = lax.scan(chain_step, jnp.zeros((GROUPS, group_heads, P_SIZE, N), jnp.float32), (states, block_decay))
    carried_in = jnp.einsum('btgn,bgqpn->btgqp', c_blocks.astype(jnp.float32), entering, precision=lax.Precision.HIGHEST)
    ssd_out = inner + jnp.exp(running)[..., None] * carried_in
    ssd_out = ssd_out.reshape(TOKENS, GROUPS, group_heads * P_SIZE)
    gated = ssd_out * jax.nn.silu(gate_input.astype(jnp.float32)).reshape(TOKENS, GROUPS, group_heads * P_SIZE)
    mean_sq = lax.optimization_barrier(jnp.mean(gated * gated, axis=-1, keepdims=True))
    normed = ((gated * lax.rsqrt(mean_sq + 1e-05)).reshape(TOKENS, HEADS * P_SIZE) * norm_gain).astype(jnp.bfloat16)
    mixer = jnp.dot(normed, out_weight, preferred_element_type=jnp.float32)
    hidden_state = (stream.astype(jnp.float32) + mixer).astype(jnp.bfloat16)
    hidden_f = hidden_state.astype(jnp.float32)
    mean_h = lax.optimization_barrier(jnp.mean(hidden_f * hidden_f, axis=-1, keepdims=True))
    expert_in = (hidden_f * lax.rsqrt(mean_h + 1e-06) * moe_gain).astype(jnp.bfloat16)
    logits = jnp.dot(expert_in, router, preferred_element_type=jnp.float32)
    scores = jax.nn.sigmoid(logits)
    picked = jnp.take_along_axis(scores, expert_ids, axis=1)
    gates = picked / lax.optimization_barrier(jnp.sum(picked, axis=1, keepdims=True))
    rows_all = N_CTX * CAP
    id_blocks = expert_ids.reshape(N_CTX, TOK_DEV * TOP)
    one_hot = (id_blocks[..., None] == jnp.arange(EXPERTS, dtype=jnp.int32)).astype(jnp.int32)
    slot_index = lax.optimization_barrier(jnp.sum((jnp.cumsum(one_hot, axis=1) - one_hot) * one_hot, axis=-1))
    target = id_blocks * rows_all + jnp.arange(N_CTX, dtype=jnp.int32)[:, None] * CAP + slot_index
    target = target.reshape(-1).astype(jnp.int32)
    token_of = (jnp.arange(TOKENS * TOP, dtype=jnp.int32) // TOP).astype(jnp.int32)
    table = jnp.full((EXPERTS * rows_all,), TOKENS, jnp.int32).at[target].set(token_of).reshape(EXPERTS, rows_all)
    gate_table = jnp.zeros((EXPERTS * rows_all,), jnp.float32).at[target].set(gates.reshape(-1)).reshape(EXPERTS, rows_all)
    padded = jnp.concatenate([expert_in, jnp.zeros((1, D), jnp.bfloat16)], axis=0)
    slice_units = FF // N_EXP

    def expert_step(total, operands):
        token_rows, gate_rows, gate_w, up_w, down_w = operands
        inputs = padded[token_rows]
        contract = (((1,), (1,)), ((), ()))
        gate_proj = lax.dot_general(inputs, gate_w, contract, preferred_element_type=jnp.float32)
        up_proj = lax.dot_general(inputs, up_w, contract, preferred_element_type=jnp.float32)
        active = (jax.nn.silu(gate_proj) * up_proj).astype(jnp.bfloat16)
        parts = jnp.einsum('rsf,sfd->rsd', active.reshape(rows_all, N_EXP, slice_units).astype(jnp.float32), down_w.reshape(N_EXP, slice_units, D).astype(jnp.float32)).astype(jnp.bfloat16)
        summed = lax.optimization_barrier(jnp.sum(parts.astype(jnp.float32), axis=1))
        return (total.at[token_rows].add(gate_rows[:, None] * summed), None)
    moe_sum, unused = lax.scan(expert_step, jnp.zeros((TOKENS + 1, D), jnp.float32), (table, gate_table, w_gate, w_up, w_down))
    return (hidden_f + moe_sum[:TOKENS]).astype(jnp.bfloat16)
```

```python
import functools

import jax
import jax.numpy as jnp
from jax import lax
from jax.experimental import pallas as pl
from jax.experimental.pallas import tpu as pltpu
from jax.sharding import PartitionSpec as P

P_SIZE = 64
N = 128
LANES = 128
SLOTS = 16
CORES = 2
MESH = pl.DeviceIdType.MESH
NT = (((1,), (1,)), ((), ()))
f32 = jnp.float32
bf16 = jnp.bfloat16


def iota(shape, dim):
    return lax.broadcasted_iota(jnp.int32, shape, dim)


def dot(a, b):
    return jnp.dot(a, b, preferred_element_type=f32)


def silu(v):
    return v / (1.0 + jnp.exp(-v))


def leading(v):
    scaled = v * 65537.0
    return scaled - (scaled - v)


def wait_bytes(ref, count, sem):
    view = ref.at[pl.ds(0, count)]
    pltpu.make_async_copy(view, view, sem).wait()


def layer_kernel(
    n_ctx,
    n_exp,
    x_ref,
    z_ref,
    b_ref,
    c_ref,
    step_ref,
    rate_ref,
    norm_gain_ref,
    out_w_hbm,
    stream_ref,
    moe_gain_ref,
    router_ref,
    ids_ref,
    w_gate_hbm,
    w_up_hbm,
    w_down_hbm,
    out_ref,
    out_w,
    w_gate,
    w_up,
    w_down,
    state_out,
    state_in,
    enter_out,
    enter_in,
    inner,
    mixed,
    mix_out,
    mix_in,
    hidden,
    expert_in,
    rows_f32,
    rows_out,
    rows_in,
    tokens,
    act,
    back_out,
    back_in,
    moe_out,
    moe_in,
    local_sem,
    ctx_send,
    ctx_recv,
    exp_send,
    exp_recv,
    w_send,
    w_recv,
):
    me_c, me_e = lax.axis_index("ctx"), lax.axis_index("exp")
    token_count, width = x_ref.shape
    head_count = step_ref.shape[0]
    pair_count = width // LANES
    part_rows = width // n_ctx
    cols = stream_ref.shape[1]
    d_model = cols * n_exp
    ff_part = w_gate_hbm.shape[0]
    ff_total = ff_part * n_exp
    per_dev = SLOTS // n_exp
    row_count = n_ctx * per_dev
    stride = per_dev * n_exp

    def ctx_peer(d):
        return lax.rem(me_c + d, n_ctx)

    def exp_peer(d):
        return lax.rem(me_e + d, n_exp)

    def to_exp(src, dst, send, recv, peer):
        return pltpu.make_async_remote_copy(
            src_ref=src,
            dst_ref=dst,
            send_sem=send,
            recv_sem=recv,
            device_id=(me_c, peer),
            device_id_type=MESH,
        )

    def exchange(src, dst, phase):
        def one(d, carry):
            peer = ctx_peer(d)
            pltpu.make_async_remote_copy(
                src_ref=src.at[peer],
                dst_ref=dst.at[me_c],
                send_sem=ctx_send.at[phase],
                recv_sem=ctx_recv.at[phase],
                device_id=(peer, me_e),
                device_id_type=MESH,
            ).start()
            return carry

        lax.fori_loop(1, n_ctx, one, 0)

    barrier = pltpu.get_barrier_semaphore()

    def greet_ctx(d, carry):
        pl.semaphore_signal(barrier, inc=1, device_id=(ctx_peer(d), me_e), device_id_type=MESH)
        return carry

    def greet_exp(d, carry):
        pl.semaphore_signal(barrier, inc=1, device_id=(me_c, exp_peer(d)), device_id_type=MESH)
        return carry

    lax.fori_loop(1, n_ctx, greet_ctx, 0)
    lax.fori_loop(1, n_exp, greet_exp, 0)

    out_w_copy = pltpu.make_async_copy(out_w_hbm, out_w, local_sem.at[0])
    out_w_copy.start()
    weights = ((w_gate_hbm, w_gate), (w_up_hbm, w_up), (w_down_hbm, w_down))

    def part(ref, index, first=0, rows=ff_part):
        return ref.at[pl.ds(pl.multiple_of(index * ff_part + first, 16), rows)]

    own_copies = [
        pltpu.make_async_copy(hbm, part(buf, me_e), local_sem.at[1 + i])
        for i, (hbm, buf) in enumerate(weights)
    ]
    for copy in own_copies:
        copy.start()

    step = step_ref[...]
    lane_t = iota((head_count, token_count), 1)
    running = -(step * rate_ref[...])
    shift = 1
    while shift < token_count:
        running = running + jnp.where(lane_t >= shift, pltpu.roll(running, shift, 1), 0.0)
        shift *= 2
    stacked = jnp.concatenate(
        [running, step, jnp.zeros((token_count - 2 * head_count, token_count), f32)], axis=0
    )
    by_token = stacked.T
    run_t = by_token[:, 0:head_count]
    step_t = by_token[:, head_count : 2 * head_count]
    last = run_t[token_count - 1 : token_count, :]
    tail = jnp.exp(last - run_t)
    grown = jnp.exp(run_t)
    total_decay = jnp.exp(last)

    first_half = iota((token_count, LANES), 1) < P_SIZE

    def expand(per_head, k):
        return jnp.where(
            first_half, per_head[:, 2 * k : 2 * k + 1], per_head[:, 2 * k + 1 : 2 * k + 2]
        )

    b_block, c_block = b_ref[...], c_ref[...]
    scores = lax.dot_general(c_block, b_block, NT, preferred_element_type=f32)
    lower = iota((token_count, token_count), 0) >= iota((token_count, token_count), 1)

    def mix_head(h, weighted):
        spread = run_t[:, h : h + 1] - running[h : h + 1, :]
        decay = jnp.where(lower, jnp.exp(jnp.where(lower, spread, 0.0)), 0.0)
        return dot((decay * scores).astype(bf16), weighted)

    row8 = iota((8, N), 0)
    for k in range(pair_count):
        lanes = slice(k * LANES, (k + 1) * LANES)
        weighted = (expand(step_t, k) * x_ref[:, lanes].astype(f32)).astype(bf16)
        inner[:, lanes] = jnp.where(
            first_half, mix_head(2 * k, weighted), mix_head(2 * k + 1, weighted)
        )
        carried = (expand(tail, k) * weighted.astype(f32)).T.astype(bf16)
        state = dot(carried, b_block)
        for i in range(LANES // part_rows):
            j = k * LANES // part_rows + i
            head = j * part_rows // P_SIZE
            decay = jnp.broadcast_to(total_decay[:, head : head + 1], (8, N))
            high = leading(decay)
            middle = leading(decay - high)
            low = decay - high - middle
            decay_rows = jnp.where(
                row8 == 0, high, jnp.where(row8 == 1, middle, jnp.where(row8 == 2, low, 0.0))
            )
            piece = state[i * part_rows : (i + 1) * part_rows, :]
            lead = leading(piece)
            state_out[j] = jnp.concatenate([lead, piece - lead, decay_rows], axis=0).astype(bf16)

    pl.semaphore_wait(barrier, n_ctx - 1 + n_exp - 1)

    exchange(state_out, state_in, 0)

    chips = n_exp // CORES
    me_x, core = me_e // CORES, lax.rem(me_e, CORES)

    def at_chip(d):
        return lax.rem(me_x + d, chips) * CORES + core

    right, left, opposite = at_chip(1), at_chip(chips - 1), at_chip(2)
    sibling = me_x * CORES + 1 - core
    half = ff_part // 32 * 16

    def send_part(buf, index, first, rows, group, arrival, peer, hbm=None):
        to_exp(
            part(buf, index, first, rows) if hbm is None else hbm,
            part(buf, index, first, rows),
            w_send.at[group],
            w_recv.at[arrival],
            peer,
        ).start()

    for hbm, buf in weights:
        send_part(buf, me_e, 0, ff_part, 0, 0, right, hbm)
        send_part(buf, me_e, 0, ff_part, 0, 1, left, hbm)
    for hbm, buf in weights:
        send_part(buf, me_e, 0, ff_part, 1, 3, sibling, hbm)

    def pass_on_neighbours():
        wait_bytes(w_gate, 3 * ff_part, w_recv.at[0])
        wait_bytes(w_gate, 3 * ff_part, w_recv.at[1])
        for _, buf in weights:
            send_part(buf, left, 0, half, 2, 2, right)
            send_part(buf, right, half, ff_part - half, 2, 2, left)
        for _, buf in weights:
            send_part(buf, left, 0, ff_part, 3, 4, sibling)
            send_part(buf, right, 0, ff_part, 3, 4, sibling)

    def pass_on_opposite():
        wait_bytes(w_gate, 3 * ff_part, w_recv.at[2])
        for _, buf in weights:
            send_part(buf, opposite, 0, ff_part, 4, 5, sibling)

    state_in[me_c] = state_out[me_c]
    wait_bytes(state_in, n_ctx - 1, ctx_recv.at[0])

    def chain(i, entering):
        enter_out[i] = entering
        block = state_in[i].astype(f32)
        r = part_rows
        terms = block[2 * r : 2 * r + 8]
        decay = terms[0:1] + terms[1:2] + terms[2:3]
        return decay * entering + (block[0:r] + block[r : 2 * r])

    lax.fori_loop(0, n_ctx, chain, jnp.zeros((part_rows, N), f32))
    exchange(enter_out, enter_in, 1)
    enter_in[me_c] = enter_out[me_c]

    lane_r = iota((token_count, row_count), 1)
    expert_of, slot_of = lax.rem(lane_r, n_ctx), lane_r // n_ctx
    named = jnp.zeros((token_count, row_count), f32)
    for k in range(ids_ref.shape[1]):
        named = named + jnp.where(ids_ref[:, k : k + 1] == expert_of, 1.0, 0.0)
    strictly = iota((token_count, token_count), 0) > iota((token_count, token_count), 1)
    rank = dot(jnp.where(strictly, 1.0, 0.0).astype(bf16), named.astype(bf16))
    wanted = (slot_of + me_e * per_dev).astype(f32)
    chosen = jnp.where(rank == wanted, named, 0.0)
    rows_of = chosen.T.astype(bf16)
    gating = [silu(z_ref[:, k * LANES : (k + 1) * LANES].astype(f32)) for k in range(pair_count)]

    wait_bytes(enter_in, n_ctx - 1, ctx_recv.at[1])
    entering = enter_in[...].reshape(width, N)
    lead = leading(entering)
    carried_in = lax.dot_general(
        c_block, lead.astype(bf16), NT, preferred_element_type=f32
    ) + lax.dot_general(
        c_block, (entering - lead).astype(bf16), NT, preferred_element_type=f32
    )
    gated = []
    for k in range(pair_count):
        lanes = slice(k * LANES, (k + 1) * LANES)
        ssd_out = inner[:, lanes] + expand(grown, k) * carried_in[:, lanes]
        gated.append(ssd_out * gating[k])
    squares = gated[0] * gated[0]
    for g in gated[1:]:
        squares = squares + g * g
    inverse = lax.rsqrt(jnp.sum(squares, axis=1, keepdims=True) / width + 1e-05)
    for k in range(pair_count):
        lanes = slice(k * LANES, (k + 1) * LANES)
        mixed[:, lanes] = (gated[k] * inverse * norm_gain_ref[:, lanes]).astype(bf16)

    out_w_copy.wait()

    def out_columns(q):
        return dot(mixed[...], out_w[:, pl.ds(pl.multiple_of(q * cols, cols), cols)])

    for d in range(1, n_exp):
        peer = exp_peer(d)
        mix_out[peer] = out_columns(peer).astype(bf16)
        to_exp(mix_out.at[peer], mix_in.at[me_e], exp_send.at[0], exp_recv.at[0], peer).start()
    own = out_columns(me_e) + stream_ref[...].astype(f32)
    wait_bytes(mix_in, n_exp - 1, exp_recv.at[0])
    for d in range(1, n_exp):
        own = own + mix_in[exp_peer(d)].astype(f32)
    hidden[me_e] = own.astype(bf16)
    for d in range(1, n_exp):
        to_exp(
            hidden.at[me_e], hidden.at[me_e], exp_send.at[1], exp_recv.at[1], exp_peer(d)
        ).start()
    wait_bytes(mix_in, n_exp - 1, exp_recv.at[1])

    tiles = [slice(i * LANES, (i + 1) * LANES) for i in range(cols // LANES)]

    def spread_rows(q, value):
        for s in range(per_dev):
            for i, lanes in enumerate(tiles):
                rows_f32.at[i][pl.ds(s * n_exp + q, n_ctx, stride=stride), :] = value[
                    s * n_ctx : (s + 1) * n_ctx, lanes
                ]

    def pack(ref):
        for i, lanes in enumerate(tiles):
            ref[:, :, lanes] = rows_f32[i].reshape(n_ctx, stride, LANES).astype(bf16)

    def unpack(ref):
        for i, lanes in enumerate(tiles):
            rows_f32[i] = ref[:, :, lanes].astype(f32).reshape(n_ctx * stride, LANES)

    def column_rows(s, q):
        return jnp.concatenate(
            [
                rows_f32.at[i][pl.ds(s * n_exp + q, n_ctx, stride=stride), :]
                for i in range(len(tiles))
            ],
            axis=1,
        ).astype(bf16)

    squares = jnp.zeros((token_count, cols), f32)
    for q in range(n_exp):
        h = hidden[q].astype(f32)
        squares = squares + h * h
    inverse = lax.rsqrt(jnp.sum(squares, axis=1, keepdims=True) / d_model + 1e-06)
    for q in range(n_exp):
        columns = slice(q * cols, (q + 1) * cols)
        value = hidden[q].astype(f32) * inverse * moe_gain_ref[:, columns]
        expert_in[:, columns] = value.astype(bf16)
        spread_rows(q, dot(rows_of, expert_in[:, columns]))
    pack(rows_out)
    exchange(rows_out, rows_in, 2)
    rows_in[me_c] = rows_out[me_c]
    pass_on_neighbours()

    logits = dot(expert_in[...], router_ref[...])
    score = 1.0 / (1.0 + jnp.exp(-logits))
    picked_score = score * named[:, 0:n_ctx]
    gate = picked_score / jnp.sum(picked_score, axis=1, keepdims=True)
    gate_rows = jnp.concatenate([gate] * per_dev, axis=1) * chosen
    gate_lead = leading(gate_rows)
    gate_high = gate_lead.astype(bf16)
    gate_low = (gate_rows - gate_lead).astype(bf16)
    pass_on_opposite()

    wait_bytes(rows_in, n_ctx - 1, ctx_recv.at[2])

    unpack(rows_in)
    for q in range(n_exp):
        for s in range(per_dev):
            tokens[s * n_ctx : (s + 1) * n_ctx, q * cols : (q + 1) * cols] = column_rows(s, q)

    for copy in own_copies:
        copy.wait()
    wait_bytes(w_gate, 3 * ff_part, w_recv.at[3])
    wait_bytes(w_gate, 6 * ff_part, w_recv.at[4])
    wait_bytes(w_gate, 3 * ff_part, w_recv.at[5])

    def hidden_units(first, count):
        units = pl.ds(first, count)
        g = lax.dot_general(tokens[...], w_gate[units, :], NT, preferred_element_type=f32)
        u = lax.dot_general(tokens[...], w_up[units, :], NT, preferred_element_type=f32)
        act[:, units] = (silu(g) * u).astype(bf16)

    chunk = min(256, ff_total)

    def units_step(i, carry):
        hidden_units(pl.multiple_of(i * chunk, chunk), chunk)
        return carry

    lax.fori_loop(0, ff_total // chunk, units_step, 0)
    if ff_total % chunk:
        hidden_units(ff_total // chunk * chunk, ff_total % chunk)

    def down_step(q, carry):
        columns = pl.ds(pl.multiple_of(q * cols, cols), cols)
        spread_rows(q, dot(act[...], w_down[:, columns]))
        return carry

    lax.fori_loop(0, n_exp, down_step, 0)
    pack(back_out)
    exchange(back_out, back_in, 3)
    back_in[me_c] = back_out[me_c]
    wait_bytes(back_in, n_ctx - 1, ctx_recv.at[3])

    unpack(back_in)

    def moe_columns(q):
        value = jnp.concatenate([column_rows(s, q) for s in range(per_dev)], axis=0)
        return dot(gate_high, value) + dot(gate_low, value)

    for d in range(1, n_exp):
        peer = exp_peer(d)
        moe_out[peer] = moe_columns(peer).astype(bf16)
        to_exp(moe_out.at[peer], moe_in.at[me_e], exp_send.at[2], exp_recv.at[2], peer).start()
    total = moe_columns(me_e) + hidden[me_e].astype(f32)
    wait_bytes(moe_in, n_exp - 1, exp_recv.at[2])
    for d in range(1, n_exp):
        total = total + moe_in[exp_peer(d)].astype(f32)
    out_ref[...] = total.astype(bf16)

    wait_bytes(state_out, n_ctx - 1, ctx_send.at[0])
    wait_bytes(enter_out, n_ctx - 1, ctx_send.at[1])
    wait_bytes(rows_out, n_ctx - 1, ctx_send.at[2])
    wait_bytes(back_out, n_ctx - 1, ctx_send.at[3])
    for phase in range(3):
        wait_bytes(mix_out, n_exp - 1, exp_send.at[phase])
    for group, slots in enumerate((6, 3, 3, 6, 3)):
        wait_bytes(w_gate, slots * ff_part, w_send.at[group])


def per_device(n_ctx, n_exp, *args):
    (x, z, b, c, step, rate, norm_gain, out_w, stream, moe_gain, router, ids, wg, wu, wd) = args
    t, width = x.shape
    cols = stream.shape[1]
    d_model = cols * n_exp
    ff_part = wg.shape[1]
    ff_total = ff_part * n_exp
    part_rows = width // n_ctx
    stride = SLOTS // n_exp * n_exp
    row_count = n_ctx * (SLOTS // n_exp)
    vmem, dma = pltpu.VMEM, pltpu.SemaphoreType.DMA
    in_vmem = pl.BlockSpec(memory_space=pltpu.VMEM)
    anywhere = pl.BlockSpec(memory_space=pl.ANY)
    specs = [in_vmem] * 7 + [anywhere] + [in_vmem] * 4 + [anywhere] * 3
    return pl.pallas_call(
        functools.partial(layer_kernel, n_ctx, n_exp),
        out_shape=jax.ShapeDtypeStruct((t, cols), bf16),
        in_specs=specs,
        out_specs=in_vmem,
        scratch_shapes=[
            vmem(out_w.shape, bf16),
            vmem((ff_total, d_model), bf16),
            vmem((ff_total, d_model), bf16),
            vmem((ff_total, d_model), bf16),
            vmem((n_ctx, 2 * part_rows + 8, N), bf16),
            vmem((n_ctx, 2 * part_rows + 8, N), bf16),
            vmem((n_ctx, part_rows, N), f32),
            vmem((n_ctx, part_rows, N), f32),
            vmem((t, width), f32),
            vmem((t, width), bf16),
            vmem((n_exp, t, cols), bf16),
            vmem((n_exp, t, cols), bf16),
            vmem((n_exp, t, cols), bf16),
            vmem((t, d_model), bf16),
            vmem((cols // LANES, n_ctx * stride, LANES), f32),
            vmem((n_ctx, stride, cols), bf16),
            vmem((n_ctx, stride, cols), bf16),
            vmem((row_count, d_model), bf16),
            vmem((row_count, ff_total), bf16),
            vmem((n_ctx, stride, cols), bf16),
            vmem((n_ctx, stride, cols), bf16),
            vmem((n_exp, t, cols), bf16),
            vmem((n_exp, t, cols), bf16),
            dma((4,)),
            dma((4,)),
            dma((4,)),
            dma((3,)),
            dma((3,)),
            dma((5,)),
            dma((6,)),
        ],
        compiler_params=pltpu.CompilerParams(
            collective_id=0, has_side_effects=True, vmem_limit_bytes=56 * 1024 * 1024
        ),
        name="layer",
    )(
        x,
        z,
        b,
        c,
        step,
        rate.reshape(-1, 1),
        norm_gain.reshape(1, -1),
        out_w,
        stream,
        moe_gain.reshape(1, -1),
        router,
        ids,
        wg[0],
        wu[0],
        wd[0],
    )


def solution(mesh):
    in_specs = (
        P("ctx", "exp"),
        P("ctx", "exp"),
        P("ctx", "exp"),
        P("ctx", "exp"),
        P("exp", "ctx"),
        P("exp"),
        P("exp"),
        P("exp", None),
        P("ctx", "exp"),
        P(),
        P(),
        P("ctx", None),
        P("ctx", "exp", None),
        P("ctx", "exp", None),
        P("ctx", "exp", None),
    )
    return jax.shard_map(
        functools.partial(per_device, mesh.shape["ctx"], mesh.shape["exp"]),
        mesh=mesh,
        in_specs=in_specs,
        out_specs=P("ctx", "exp"),
        check_vma=False,
    )
```

```python
import functools

import jax
import jax.numpy as jnp
from jax import lax
from jax.experimental import pallas as pl
from jax.experimental.pallas import tpu as pltpu
from jax.sharding import PartitionSpec as P

P_SIZE = 64
N = 128
LANES = 128
SLOTS = 16
CORES = 2
MESH = pl.DeviceIdType.MESH
NT = (((1,), (1,)), ((), ()))
f32 = jnp.float32
bf16 = jnp.bfloat16


def iota(shape, dim):
    return lax.broadcasted_iota(jnp.int32, shape, dim)


def dot(a, b):
    return jnp.dot(a, b, preferred_element_type=f32)


def silu(v):
    return v / (1.0 + jnp.exp(-v))


def leading(v):
    scaled = v * 65537.0
    return scaled - (scaled - v)


def wait_bytes(ref, count, sem):
    view = ref.at[pl.ds(0, count)]
    pltpu.make_async_copy(view, view, sem).wait()


def layer_kernel(
    n_ctx,
    n_exp,
    x_hbm,
    z_hbm,
    b_hbm,
    c_hbm,
    step_hbm,
    rate_hbm,
    norm_gain_hbm,
    out_w_hbm,
    stream_hbm,
    moe_gain_hbm,
    router_hbm,
    ids_hbm,
    w_gate_hbm,
    w_up_hbm,
    w_down_hbm,
    out_ref,
    x_ref,
    z_ref,
    b_ref,
    c_ref,
    step_ref,
    rate_ref,
    norm_gain_ref,
    out_w,
    stream_ref,
    moe_gain_ref,
    router_ref,
    ids_ref,
    w_gate,
    w_up,
    w_down,
    state_out,
    state_in,
    enter_out,
    enter_in,
    inner,
    mixed,
    mix_out,
    mix_in,
    hidden,
    expert_in,
    rows_f32,
    rows_out,
    rows_in,
    tokens,
    act,
    back_out,
    back_in,
    moe_out,
    moe_in,
    local_sem,
    ctx_send,
    ctx_recv,
    exp_send,
    exp_recv,
    w_send,
    w_recv,
):
    me_c, me_e = lax.axis_index("ctx"), lax.axis_index("exp")
    token_count, width = x_ref.shape
    head_count = step_ref.shape[0]
    pair_count = width // LANES
    part_rows = width // n_ctx
    cols = stream_ref.shape[1]
    d_model = cols * n_exp
    ff_part = w_gate_hbm.shape[0]
    ff_total = ff_part * n_exp
    per_dev = SLOTS // n_exp
    row_count = n_ctx * per_dev
    stride = per_dev * n_exp

    def ctx_peer(d):
        odd, away = lax.rem(d, 2), (d + 1) // 2
        return lax.rem(me_c + odd * away + (1 - odd) * (n_ctx - away), n_ctx)

    far_first = sorted(range(1, n_exp), key=lambda d: (abs(d - n_exp // 2), d))

    def exp_peer(d):
        return lax.rem(me_e + d, n_exp)

    def to_exp(src, dst, send, recv, peer):
        return pltpu.make_async_remote_copy(
            src_ref=src,
            dst_ref=dst,
            send_sem=send,
            recv_sem=recv,
            device_id=(me_c, peer),
            device_id_type=MESH,
        )

    def exchange(src, dst, phase):
        def one(d, carry):
            peer = ctx_peer(d)
            pltpu.make_async_remote_copy(
                src_ref=src.at[peer],
                dst_ref=dst.at[me_c],
                send_sem=ctx_send.at[phase],
                recv_sem=ctx_recv.at[phase],
                device_id=(peer, me_e),
                device_id_type=MESH,
            ).start()
            return carry

        lax.fori_loop(1, n_ctx, one, 0)

    barrier = pltpu.get_barrier_semaphore()

    def greet_ctx(d, carry):
        pl.semaphore_signal(barrier, inc=1, device_id=(ctx_peer(d), me_e), device_id_type=MESH)
        return carry

    def greet_exp(d, carry):
        pl.semaphore_signal(barrier, inc=1, device_id=(me_c, exp_peer(d)), device_id_type=MESH)
        return carry

    lax.fori_loop(1, n_ctx, greet_ctx, 0)
    lax.fori_loop(1, n_exp, greet_exp, 0)

    fetched = [
        pltpu.make_async_copy(hbm, vmem, local_sem.at[3 + i])
        for i, (hbm, vmem) in enumerate(
            (
                (step_hbm, step_ref),
                (rate_hbm, rate_ref),
                (x_hbm, x_ref),
                (b_hbm, b_ref),
                (c_hbm, c_ref),
                (z_hbm, z_ref),
                (ids_hbm, ids_ref),
                (norm_gain_hbm, norm_gain_ref),
                (stream_hbm, stream_ref),
                (moe_gain_hbm, moe_gain_ref),
                (router_hbm, router_ref),
                (out_w_hbm, out_w),
            )
        )
    ]
    for copy in fetched:
        copy.start()
    weights = ((w_gate_hbm, w_gate), (w_up_hbm, w_up), (w_down_hbm, w_down))

    def part(ref, index, first=0, rows=ff_part):
        return ref.at[pl.ds(pl.multiple_of(index * ff_part + first, 16), rows)]

    own_copies = [
        pltpu.make_async_copy(hbm, part(buf, me_e), local_sem.at[i])
        for i, (hbm, buf) in enumerate(weights)
    ]
    for copy in own_copies:
        copy.start()

    for copy in fetched[0:4]:
        copy.wait()
    step = step_ref[...]
    diagonal = iota((head_count, head_count), 0) == iota((head_count, head_count), 1)
    rate = jnp.sum(jnp.where(diagonal, rate_ref[...], 0.0), axis=1, keepdims=True)
    lane_t = iota((head_count, token_count), 1)
    running = -(step * rate)
    shift = 1
    while shift < token_count:
        running = running + jnp.where(lane_t >= shift, pltpu.roll(running, shift, 1), 0.0)
        shift *= 2
    stacked = jnp.concatenate(
        [running, step, jnp.zeros((token_count - 2 * head_count, token_count), f32)], axis=0
    )
    by_token = stacked.T
    run_t = by_token[:, 0:head_count]
    step_t = by_token[:, head_count : 2 * head_count]
    last = run_t[token_count - 1 : token_count, :]
    tail = jnp.exp(last - run_t)
    grown = jnp.exp(run_t)
    total_decay = jnp.exp(last)

    first_half = iota((token_count, LANES), 1) < P_SIZE

    def expand(per_head, k):
        return jnp.where(
            first_half, per_head[:, 2 * k : 2 * k + 1], per_head[:, 2 * k + 1 : 2 * k + 2]
        )

    b_block = b_ref[...]
    row8 = iota((8, N), 0)
    weighted = []
    for k in range(pair_count):
        lanes = slice(k * LANES, (k + 1) * LANES)
        stepped = (expand(step_t, k) * x_ref[:, lanes].astype(f32)).astype(bf16)
        weighted.append(stepped)
        carried = (expand(tail, k) * stepped.astype(f32)).T.astype(bf16)
        state = dot(carried, b_block)
        for i in range(LANES // part_rows):
            j = k * LANES // part_rows + i
            head = j * part_rows // P_SIZE
            decay = jnp.broadcast_to(total_decay[:, head : head + 1], (8, N))
            high = leading(decay)
            middle = leading(decay - high)
            low = decay - high - middle
            decay_rows = jnp.where(
                row8 == 0, high, jnp.where(row8 == 1, middle, jnp.where(row8 == 2, low, 0.0))
            )
            piece = state[i * part_rows : (i + 1) * part_rows, :]
            lead = leading(piece)
            state_out[j] = jnp.concatenate([lead, piece - lead, decay_rows], axis=0).astype(bf16)

    pl.semaphore_wait(barrier, n_ctx - 1 + n_exp - 1)

    exchange(state_out, state_in, 0)

    chips = n_exp // CORES
    me_x, core = me_e // CORES, lax.rem(me_e, CORES)

    def at_chip(d):
        return lax.rem(me_x + d, chips) * CORES + core

    right, left, opposite = at_chip(1), at_chip(chips - 1), at_chip(2)
    sibling = me_x * CORES + 1 - core
    half = ff_part // 32 * 16

    def send_part(i, index, first, rows, group, arrival, peer, hbm=None):
        buf = weights[i][1]
        to_exp(
            part(buf, index, first, rows) if hbm is None else hbm,
            part(buf, index, first, rows),
            w_send.at[i, group],
            w_recv.at[i, arrival],
            peer,
        ).start()

    def arrived(i, arrival, slots):
        wait_bytes(w_gate, slots * ff_part, w_recv.at[i, arrival])

    def send_own(i):
        hbm = weights[i][0]
        send_part(i, me_e, 0, ff_part, 0, 0, right, hbm)
        send_part(i, me_e, 0, ff_part, 0, 1, left, hbm)
        send_part(i, me_e, 0, ff_part, 1, 3, sibling, hbm)

    def pass_on_neighbours(i):
        arrived(i, 0, 1)
        arrived(i, 1, 1)
        send_part(i, left, 0, half, 2, 2, right)
        send_part(i, right, half, ff_part - half, 2, 2, left)
        send_part(i, left, 0, ff_part, 3, 4, sibling)
        send_part(i, right, 0, ff_part, 3, 4, sibling)

    def pass_on_opposite(i):
        arrived(i, 2, 1)
        send_part(i, opposite, 0, ff_part, 4, 5, sibling)

    def complete(i):
        own_copies[i].wait()
        arrived(i, 3, 1)
        arrived(i, 4, 2)
        arrived(i, 5, 1)

    send_own(0)
    send_own(1)

    fetched[4].wait()
    c_block = c_ref[...]
    scores = lax.dot_general(c_block, b_block, NT, preferred_element_type=f32)
    lower = iota((token_count, token_count), 0) >= iota((token_count, token_count), 1)

    def mix_head(h, values):
        spread = run_t[:, h : h + 1] - running[h : h + 1, :]
        decay = jnp.where(lower, jnp.exp(jnp.where(lower, spread, 0.0)), 0.0)
        return dot((decay * scores).astype(bf16), values)

    for k in range(pair_count):
        inner[:, k * LANES : (k + 1) * LANES] = jnp.where(
            first_half, mix_head(2 * k, weighted[k]), mix_head(2 * k + 1, weighted[k])
        )

    state_in[me_c] = state_out[me_c]
    wait_bytes(state_in, n_ctx - 1, ctx_recv.at[0])

    def chain(i, entering):
        enter_out[i] = entering
        block = state_in[i].astype(f32)
        r = part_rows
        terms = block[2 * r : 2 * r + 8]
        decay = terms[0:1] + terms[1:2] + terms[2:3]
        return decay * entering + (block[0:r] + block[r : 2 * r])

    lax.fori_loop(0, n_ctx, chain, jnp.zeros((part_rows, N), f32), unroll=min(8, n_ctx))
    exchange(enter_out, enter_in, 1)
    enter_in[me_c] = enter_out[me_c]
    pass_on_neighbours(0)

    for copy in fetched[5:]:
        copy.wait()
    row_r = iota((row_count, token_count), 0)
    expert_of, slot_of = lax.rem(row_r, n_ctx), row_r // n_ctx
    named = jnp.zeros((row_count, token_count), f32)
    for k in range(ids_ref.shape[0]):
        named = named + jnp.where(ids_ref[k : k + 1, :] == expert_of, 1.0, 0.0)
    earlier = iota((token_count, token_count), 0) < iota((token_count, token_count), 1)
    rank = dot(named.astype(bf16), jnp.where(earlier, 1.0, 0.0).astype(bf16))
    wanted = (slot_of + me_e * per_dev).astype(f32)
    chosen = jnp.where(rank == wanted, named, 0.0)
    rows_of = chosen.astype(bf16)
    gating = [silu(z_ref[:, k * LANES : (k + 1) * LANES].astype(f32)) for k in range(pair_count)]

    wait_bytes(enter_in, n_ctx - 1, ctx_recv.at[1])
    entering = enter_in[...].reshape(width, N)
    lead = leading(entering)
    carried_in = lax.dot_general(
        c_block, lead.astype(bf16), NT, preferred_element_type=f32
    ) + lax.dot_general(
        c_block, (entering - lead).astype(bf16), NT, preferred_element_type=f32
    )
    gated = []
    for k in range(pair_count):
        lanes = slice(k * LANES, (k + 1) * LANES)
        ssd_out = inner[:, lanes] + expand(grown, k) * carried_in[:, lanes]
        gated.append(ssd_out * gating[k])
    squares = gated[0] * gated[0]
    for g in gated[1:]:
        squares = squares + g * g
    inverse = lax.rsqrt(jnp.sum(squares, axis=1, keepdims=True) / width + 1e-05)
    for k in range(pair_count):
        lanes = slice(k * LANES, (k + 1) * LANES)
        mixed[:, lanes] = (gated[k] * inverse * norm_gain_ref[:, lanes]).astype(bf16)

    def out_columns(q):
        return dot(mixed[...], out_w[:, pl.ds(pl.multiple_of(q * cols, cols), cols)])

    for d in far_first:
        peer = exp_peer(d)
        mix_out[peer] = out_columns(peer).astype(bf16)
        to_exp(mix_out.at[peer], mix_in.at[me_e], exp_send.at[0], exp_recv.at[0], peer).start()
    own = out_columns(me_e) + stream_ref[...].astype(f32)
    wait_bytes(mix_in, n_exp - 1, exp_recv.at[0])
    for d in range(1, n_exp):
        own = own + mix_in[exp_peer(d)].astype(f32)
    hidden[me_e] = own.astype(bf16)
    for d in far_first:
        to_exp(
            hidden.at[me_e], hidden.at[me_e], exp_send.at[1], exp_recv.at[1], exp_peer(d)
        ).start()
    wait_bytes(mix_in, n_exp - 1, exp_recv.at[1])

    tiles = [slice(i * LANES, (i + 1) * LANES) for i in range(cols // LANES)]

    def spread_rows(q, value):
        for s in range(per_dev):
            for i, lanes in enumerate(tiles):
                rows_f32.at[i][pl.ds(s * n_exp + q, n_ctx, stride=stride), :] = value[
                    s * n_ctx : (s + 1) * n_ctx, lanes
                ]

    def pack(ref):
        for i, lanes in enumerate(tiles):
            ref[:, :, lanes] = rows_f32[i].reshape(n_ctx, stride, LANES).astype(bf16)

    def unpack(ref):
        for i, lanes in enumerate(tiles):
            rows_f32[i] = ref[:, :, lanes].astype(f32).reshape(n_ctx * stride, LANES)

    def column_rows(s, q):
        return jnp.concatenate(
            [
                rows_f32.at[i][pl.ds(s * n_exp + q, n_ctx, stride=stride), :]
                for i in range(len(tiles))
            ],
            axis=1,
        ).astype(bf16)

    send_own(2)
    pass_on_neighbours(1)
    pass_on_opposite(0)
    squares = jnp.zeros((token_count, cols), f32)
    for q in range(n_exp):
        h = hidden[q].astype(f32)
        squares = squares + h * h
    inverse = lax.rsqrt(jnp.sum(squares, axis=1, keepdims=True) / d_model + 1e-06)
    for q in range(n_exp):
        columns = slice(q * cols, (q + 1) * cols)
        value = hidden[q].astype(f32) * inverse * moe_gain_ref[:, columns]
        expert_in[:, columns] = value.astype(bf16)
        spread_rows(q, dot(rows_of, expert_in[:, columns]))
    pack(rows_out)
    exchange(rows_out, rows_in, 2)
    rows_in[me_c] = rows_out[me_c]

    logits = lax.dot_general(expert_in[...], router_ref[...], NT, preferred_element_type=f32)
    named_t, chosen_t = named.T, chosen.T
    score = 1.0 / (1.0 + jnp.exp(-logits))
    picked_score = score * named_t[:, 0:n_ctx]
    gate = picked_score / jnp.sum(picked_score, axis=1, keepdims=True)
    gate_rows = jnp.concatenate([gate] * per_dev, axis=1) * chosen_t
    gate_lead = leading(gate_rows)
    gate_high = gate_lead.astype(bf16)
    gate_low = (gate_rows - gate_lead).astype(bf16)
    pass_on_neighbours(2)
    pass_on_opposite(1)

    wait_bytes(rows_in, n_ctx - 1, ctx_recv.at[2])

    unpack(rows_in)
    for q in range(n_exp):
        for s in range(per_dev):
            tokens[s * n_ctx : (s + 1) * n_ctx, q * cols : (q + 1) * cols] = column_rows(s, q)

    complete(0)
    complete(1)
    pass_on_opposite(2)

    def hidden_units(first, count):
        units = pl.ds(first, count)
        g = lax.dot_general(tokens[...], w_gate[units, :], NT, preferred_element_type=f32)
        u = lax.dot_general(tokens[...], w_up[units, :], NT, preferred_element_type=f32)
        act[:, units] = (silu(g) * u).astype(bf16)

    chunk = min(256, ff_total)

    def units_step(i, carry):
        hidden_units(pl.multiple_of(i * chunk, chunk), chunk)
        return carry

    lax.fori_loop(0, ff_total // chunk, units_step, 0)
    if ff_total % chunk:
        hidden_units(ff_total // chunk * chunk, ff_total % chunk)

    complete(2)

    def down_step(q, carry):
        columns = pl.ds(pl.multiple_of(q * cols, cols), cols)
        spread_rows(q, dot(act[...], w_down[:, columns]))
        return carry

    lax.fori_loop(0, n_exp, down_step, 0)
    pack(back_out)
    exchange(back_out, back_in, 3)
    back_in[me_c] = back_out[me_c]
    wait_bytes(back_in, n_ctx - 1, ctx_recv.at[3])

    unpack(back_in)

    def moe_columns(q):
        value = jnp.concatenate([column_rows(s, q) for s in range(per_dev)], axis=0)
        return dot(gate_high, value) + dot(gate_low, value)

    for d in far_first:
        peer = exp_peer(d)
        moe_out[peer] = moe_columns(peer).astype(bf16)
        to_exp(moe_out.at[peer], moe_in.at[me_e], exp_send.at[2], exp_recv.at[2], peer).start()
    total = moe_columns(me_e) + hidden[me_e].astype(f32)
    wait_bytes(moe_in, n_exp - 1, exp_recv.at[2])
    for d in range(1, n_exp):
        total = total + moe_in[exp_peer(d)].astype(f32)
    out_ref[...] = total.astype(bf16)

    wait_bytes(state_out, n_ctx - 1, ctx_send.at[0])
    wait_bytes(enter_out, n_ctx - 1, ctx_send.at[1])
    wait_bytes(rows_out, n_ctx - 1, ctx_send.at[2])
    wait_bytes(back_out, n_ctx - 1, ctx_send.at[3])
    for phase in range(3):
        wait_bytes(mix_out, n_exp - 1, exp_send.at[phase])
    for i in range(3):
        for group, slots in enumerate((2, 1, 1, 2, 1)):
            wait_bytes(w_gate, slots * ff_part, w_send.at[i, group])


def per_device(n_ctx, n_exp, *args):
    (x, z, b, c, step, rate, norm_gain, out_w, stream, moe_gain, router, ids, wg, wu, wd) = args
    t, width = x.shape
    cols = stream.shape[1]
    d_model = cols * n_exp
    ff_part = wg.shape[1]
    ff_total = ff_part * n_exp
    part_rows = width // n_ctx
    stride = SLOTS // n_exp * n_exp
    row_count = n_ctx * (SLOTS // n_exp)
    vmem, dma = pltpu.VMEM, pltpu.SemaphoreType.DMA
    anywhere = pl.BlockSpec(memory_space=pl.ANY)
    rate, norm_gain, moe_gain = (v.reshape(1, -1) for v in (rate, norm_gain, moe_gain))
    router, ids = router.T, ids.T
    inputs = (x, z, b, c, step, rate, norm_gain, out_w, stream, moe_gain, router, ids)
    return pl.pallas_call(
        functools.partial(layer_kernel, n_ctx, n_exp),
        out_shape=jax.ShapeDtypeStruct((t, cols), bf16),
        in_specs=[anywhere] * 15,
        out_specs=pl.BlockSpec(memory_space=pltpu.VMEM),
        scratch_shapes=[
            *(vmem(v.shape, v.dtype) for v in inputs),
            vmem((ff_total, d_model), bf16),
            vmem((ff_total, d_model), bf16),
            vmem((ff_total, d_model), bf16),
            vmem((n_ctx, 2 * part_rows + 8, N), bf16),
            vmem((n_ctx, 2 * part_rows + 8, N), bf16),
            vmem((n_ctx, part_rows, N), f32),
            vmem((n_ctx, part_rows, N), f32),
            vmem((t, width), f32),
            vmem((t, width), bf16),
            vmem((n_exp, t, cols), bf16),
            vmem((n_exp, t, cols), bf16),
            vmem((n_exp, t, cols), bf16),
            vmem((t, d_model), bf16),
            vmem((cols // LANES, n_ctx * stride, LANES), f32),
            vmem((n_ctx, stride, cols), bf16),
            vmem((n_ctx, stride, cols), bf16),
            vmem((row_count, d_model), bf16),
            vmem((row_count, ff_total), bf16),
            vmem((n_ctx, stride, cols), bf16),
            vmem((n_ctx, stride, cols), bf16),
            vmem((n_exp, t, cols), bf16),
            vmem((n_exp, t, cols), bf16),
            dma((15,)),
            dma((4,)),
            dma((4,)),
            dma((3,)),
            dma((3,)),
            dma((3, 5)),
            dma((3, 6)),
        ],
        compiler_params=pltpu.CompilerParams(
            collective_id=0, has_side_effects=True, vmem_limit_bytes=56 * 1024 * 1024
        ),
        name="layer",
    )(
        *inputs,
        wg[0],
        wu[0],
        wd[0],
    )


def solution(mesh):
    in_specs = (
        P("ctx", "exp"),
        P("ctx", "exp"),
        P("ctx", "exp"),
        P("ctx", "exp"),
        P("exp", "ctx"),
        P("exp"),
        P("exp"),
        P("exp", None),
        P("ctx", "exp"),
        P(),
        P(),
        P("ctx", None),
        P("ctx", "exp", None),
        P("ctx", "exp", None),
        P("ctx", "exp", None),
    )
    return jax.shard_map(
        functools.partial(per_device, mesh.shape["ctx"], mesh.shape["exp"]),
        mesh=mesh,
        in_specs=in_specs,
        out_specs=P("ctx", "exp"),
        check_vma=False,
    )
```

```python
import functools

import jax
import jax.numpy as jnp
from jax import lax
from jax.experimental import pallas as pl
from jax.experimental.pallas import tpu as pltpu
from jax.sharding import PartitionSpec as P

P_SIZE = 64
N = 128
LANES = 128
SLOTS = 16
PARTS = 2
CORES = 2
MESH = pl.DeviceIdType.MESH
NT = (((1,), (1,)), ((), ()))
f32 = jnp.float32
bf16 = jnp.bfloat16


def iota(shape, dim):
    return lax.broadcasted_iota(jnp.int32, shape, dim)


def dot(a, b):
    return jnp.dot(a, b, preferred_element_type=f32)


def silu(v):
    return v / (1.0 + jnp.exp(-v))


def leading(v):
    scaled = v * 65537.0
    return scaled - (scaled - v)


def wait_bytes(ref, count, sem):
    view = ref.at[pl.ds(0, count)]
    pltpu.make_async_copy(view, view, sem).wait()


def layer_kernel(
    n_ctx,
    n_exp,
    x_hbm,
    z_hbm,
    b_hbm,
    c_hbm,
    step_hbm,
    rate_hbm,
    norm_gain_hbm,
    out_w_hbm,
    stream_hbm,
    moe_gain_hbm,
    router_hbm,
    ids_hbm,
    w_gate_hbm,
    w_up_hbm,
    w_down_hbm,
    out_ref,
    x_ref,
    z_ref,
    b_ref,
    c_ref,
    step_ref,
    rate_ref,
    norm_gain_ref,
    out_w,
    stream_ref,
    moe_gain_ref,
    router_ref,
    ids_ref,
    w_gate,
    w_up,
    w_down,
    state_out,
    state_in,
    decay_out,
    decay_in,
    enter_out,
    enter_in,
    inner,
    mixed,
    mix_out,
    mix_in,
    hidden,
    expert_in,
    rows_f32,
    rows_out,
    rows_in,
    tokens,
    act,
    back_out,
    back_in,
    moe_out,
    moe_in,
    local_sem,
    ctx_send,
    ctx_recv,
    exp_send,
    exp_recv,
    pair_recv,
    hidden_recv,
    w_send,
    w_recv,
):
    me_c, me_e = lax.axis_index("ctx"), lax.axis_index("exp")
    token_count, width = x_ref.shape
    head_count = step_ref.shape[0]
    pair_count = width // LANES
    part_rows = width // n_ctx
    cols = stream_ref.shape[1]
    d_model = cols * n_exp
    ff_part = w_gate_hbm.shape[0]
    ff_total = ff_part * n_exp
    per_dev = SLOTS // n_exp
    row_count = n_ctx * per_dev

    def ctx_peer(d):
        odd, away = lax.rem(d, 2), (d + 1) // 2
        return lax.rem(me_c + odd * away + (1 - odd) * (n_ctx - away), n_ctx)


    def exp_peer(d):
        return lax.rem(me_e + d, n_exp)

    def to_exp(src, dst, send, recv, peer):
        return pltpu.make_async_remote_copy(
            src_ref=src,
            dst_ref=dst,
            send_sem=send,
            recv_sem=recv,
            device_id=(me_c, peer),
            device_id_type=MESH,
        )

    def exchange(src, dst, phase, entry=lambda peer: peer):
        def one(d, carry):
            peer = ctx_peer(d)
            pltpu.make_async_remote_copy(
                src_ref=src.at[entry(peer)],
                dst_ref=dst.at[me_c],
                send_sem=ctx_send.at[phase],
                recv_sem=ctx_recv.at[phase],
                device_id=(peer, me_e),
                device_id_type=MESH,
            ).start()
            return carry

        lax.fori_loop(1, n_ctx, one, 0, unroll=3 if n_ctx % 3 == 1 else 1)

    barrier = pltpu.get_barrier_semaphore()

    def greet_ctx(d, carry):
        pl.semaphore_signal(barrier, inc=1, device_id=(ctx_peer(d), me_e), device_id_type=MESH)
        return carry

    def greet_exp(d, carry):
        pl.semaphore_signal(barrier, inc=1, device_id=(me_c, exp_peer(d)), device_id_type=MESH)
        return carry

    lax.fori_loop(1, n_ctx, greet_ctx, 0)
    lax.fori_loop(1, n_exp, greet_exp, 0)

    fetched = [
        pltpu.make_async_copy(hbm, vmem, local_sem.at[3 + i])
        for i, (hbm, vmem) in enumerate(
            (
                (step_hbm, step_ref),
                (rate_hbm, rate_ref),
                (x_hbm, x_ref),
                (b_hbm, b_ref),
                (c_hbm, c_ref),
                (z_hbm, z_ref),
                (ids_hbm, ids_ref),
                (norm_gain_hbm, norm_gain_ref),
                (stream_hbm, stream_ref),
                (moe_gain_hbm, moe_gain_ref),
                (router_hbm, router_ref),
                (out_w_hbm, out_w),
            )
        )
    ]
    for copy in fetched:
        copy.start()
    weights = ((w_gate_hbm, w_gate), (w_up_hbm, w_up), (w_down_hbm, w_down))

    def part(ref, index, first=0, rows=ff_part):
        return ref.at[pl.ds(pl.multiple_of(index * ff_part + first, 16), rows)]

    own_copies = [
        pltpu.make_async_copy(hbm, part(buf, me_e), local_sem.at[i])
        for i, (hbm, buf) in enumerate(weights)
    ]
    for copy in own_copies:
        copy.start()

    for copy in fetched[0:4]:
        copy.wait()
    step = step_ref[...]
    diagonal = iota((head_count, head_count), 0) == iota((head_count, head_count), 1)
    rate = jnp.sum(jnp.where(diagonal, rate_ref[...], 0.0), axis=1, keepdims=True)
    lane_t = iota((head_count, token_count), 1)
    running = -(step * rate)
    shift = 1
    while shift < token_count:
        running = running + jnp.where(lane_t >= shift, pltpu.roll(running, shift, 1), 0.0)
        shift *= 2
    stacked = jnp.concatenate(
        [running, step, jnp.zeros((token_count - 2 * head_count, token_count), f32)], axis=0
    )
    by_token = stacked.T
    run_t = by_token[:, 0:head_count]
    step_t = by_token[:, head_count : 2 * head_count]
    last = run_t[token_count - 1 : token_count, :]
    tail = jnp.exp(last - run_t)
    grown = jnp.exp(run_t)
    total_decay = jnp.exp(last)
    for h in range(head_count):
        decay_out[h] = jnp.broadcast_to(total_decay[:, h : h + 1], (1, N))

    first_half = iota((token_count, LANES), 1) < P_SIZE

    def expand(per_head, k):
        return jnp.where(
            first_half, per_head[:, 2 * k : 2 * k + 1], per_head[:, 2 * k + 1 : 2 * k + 2]
        )

    b_block = b_ref[...]
    weighted = []
    for k in range(pair_count):
        lanes = slice(k * LANES, (k + 1) * LANES)
        stepped = (expand(step_t, k) * x_ref[:, lanes].astype(f32)).astype(bf16)
        weighted.append(stepped)
        carried = (expand(tail, k) * stepped.astype(f32)).T.astype(bf16)
        state = dot(carried, b_block)
        for i in range(LANES // part_rows):
            j = k * LANES // part_rows + i
            piece = state[i * part_rows : (i + 1) * part_rows, :]
            lead = leading(piece)
            state_out[j] = jnp.concatenate([lead, piece - lead], axis=0).astype(bf16)

    pl.semaphore_wait(barrier, n_ctx - 1 + n_exp - 1)

    exchange(state_out, state_in, 0)
    exchange(decay_out, decay_in, 6, lambda peer: peer * part_rows // P_SIZE)

    chips = n_exp // CORES
    me_x, core = me_e // CORES, lax.rem(me_e, CORES)

    def at_chip(d):
        return lax.rem(me_x + d, chips) * CORES + core

    right, left, opposite = at_chip(1), at_chip(chips - 1), at_chip(2)
    sibling = me_x * CORES + 1 - core
    half = ff_part // 32 * 16

    def send_part(i, index, first, rows, group, arrival, peer, hbm=None):
        buf = weights[i][1]
        to_exp(
            part(buf, index, first, rows) if hbm is None else hbm,
            part(buf, index, first, rows),
            w_send.at[i, group],
            w_recv.at[i, arrival],
            peer,
        ).start()

    def arrived(i, arrival, slots):
        wait_bytes(w_gate, slots * ff_part, w_recv.at[i, arrival])

    def send_own(i):
        hbm = weights[i][0]
        send_part(i, me_e, 0, ff_part, 0, 0, right, hbm)
        send_part(i, me_e, 0, ff_part, 0, 1, left, hbm)
        send_part(i, me_e, 0, ff_part, 1, 3, sibling, hbm)

    def pass_on_neighbours(i):
        arrived(i, 0, 1)
        arrived(i, 1, 1)
        send_part(i, left, 0, half, 2, 2, right)
        send_part(i, right, half, ff_part - half, 2, 2, left)
        send_part(i, left, 0, ff_part, 3, 4, sibling)
        send_part(i, right, 0, ff_part, 3, 4, sibling)

    def pass_on_opposite(i):
        arrived(i, 2, 1)
        send_part(i, opposite, 0, ff_part, 4, 5, sibling)

    def complete(i):
        own_copies[i].wait()
        arrived(i, 3, 1)
        arrived(i, 4, 2)
        arrived(i, 5, 1)

    send_own(0)
    send_own(1)

    fetched[4].wait()
    c_block = c_ref[...]
    scores = lax.dot_general(c_block, b_block, NT, preferred_element_type=f32)
    lower = iota((token_count, token_count), 0) >= iota((token_count, token_count), 1)

    def mix_head(h, values):
        spread = run_t[:, h : h + 1] - running[h : h + 1, :]
        decay = jnp.where(lower, jnp.exp(jnp.where(lower, spread, 0.0)), 0.0)
        return dot((decay * scores).astype(bf16), values)

    for k in range(pair_count):
        inner[:, k * LANES : (k + 1) * LANES] = jnp.where(
            first_half, mix_head(2 * k, weighted[k]), mix_head(2 * k + 1, weighted[k])
        )

    state_in[me_c] = state_out[me_c]
    decay_in[me_c] = decay_out[me_c * part_rows // P_SIZE]
    wait_bytes(state_in, n_ctx - 1, ctx_recv.at[0])
    wait_bytes(decay_in, n_ctx - 1, ctx_recv.at[6])

    def chain(i, entering):
        enter_out[i] = entering
        block = state_in[i].astype(f32)
        r = part_rows
        return decay_in[i] * entering + (block[0:r] + block[r : 2 * r])

    lax.fori_loop(0, n_ctx, chain, jnp.zeros((part_rows, N), f32), unroll=min(8, n_ctx))
    exchange(enter_out, enter_in, 1)
    enter_in[me_c] = enter_out[me_c]

    for copy in fetched[5:]:
        copy.wait()
    row_r = iota((row_count, token_count), 0)
    expert_of, slot_of = lax.rem(row_r, n_ctx), row_r // n_ctx
    named = jnp.zeros((row_count, token_count), f32)
    for k in range(ids_ref.shape[0]):
        named = named + jnp.where(ids_ref[k : k + 1, :] == expert_of, 1.0, 0.0)
    earlier = iota((token_count, token_count), 0) < iota((token_count, token_count), 1)
    rank = dot(named.astype(bf16), jnp.where(earlier, 1.0, 0.0).astype(bf16))
    wanted = (slot_of + me_e * per_dev).astype(f32)
    chosen = jnp.where(rank == wanted, named, 0.0)
    rows_of = chosen.astype(bf16)
    gating = [silu(z_ref[:, k * LANES : (k + 1) * LANES].astype(f32)) for k in range(pair_count)]

    pass_on_neighbours(0)

    wait_bytes(enter_in, n_ctx - 1, ctx_recv.at[1])
    entering = enter_in[...].reshape(width, N)
    lead = leading(entering)
    carried_in = lax.dot_general(
        c_block, lead.astype(bf16), NT, preferred_element_type=f32
    ) + lax.dot_general(
        c_block, (entering - lead).astype(bf16), NT, preferred_element_type=f32
    )
    gated = []
    for k in range(pair_count):
        lanes = slice(k * LANES, (k + 1) * LANES)
        ssd_out = inner[:, lanes] + expand(grown, k) * carried_in[:, lanes]
        gated.append(ssd_out * gating[k])
    squares = gated[0] * gated[0]
    for g in gated[1:]:
        squares = squares + g * g
    inverse = lax.rsqrt(jnp.sum(squares, axis=1, keepdims=True) / width + 1e-05)
    for k in range(pair_count):
        lanes = slice(k * LANES, (k + 1) * LANES)
        mixed[:, lanes] = (gated[k] * inverse * norm_gain_ref[:, lanes]).astype(bf16)

    def out_columns(q):
        return dot(mixed[...], out_w[:, pl.ds(pl.multiple_of(q * cols, cols), cols)])

    away = (2, 1, 3)
    for r in (*away, 0):
        chip = lax.rem(me_x + r, chips)
        mix_out[r] = out_columns(chip * CORES + 1 - core).astype(bf16)
        to_exp(mix_out.at[r], mix_in.at[r], exp_send.at[0], pair_recv.at[r], sibling).start()

    def pair_columns(r):
        value = out_columns(at_chip(r))
        wait_bytes(mix_in, 1, pair_recv.at[r])
        return value + mix_in[r].astype(f32)

    for r in away:
        mix_out[chips + r] = pair_columns(r).astype(bf16)
        to_exp(
            mix_out.at[chips + r],
            mix_in.at[2 * chips - r],
            exp_send.at[1],
            exp_recv.at[0],
            at_chip(r),
        ).start()
    own = pair_columns(0) + stream_ref[...].astype(f32)
    wait_bytes(mix_in, chips - 1, exp_recv.at[0])
    for r in away:
        own = own + mix_in[chips + r].astype(f32)

    hidden[me_e] = own.astype(bf16)
    mine = hidden.at[me_e]
    for r in away:
        to_exp(mine, mine, exp_send.at[3], hidden_recv.at[chips - r], at_chip(r)).start()
    to_exp(mine, mine, exp_send.at[3], hidden_recv.at[0], sibling).start()
    for r in (1, 3, 2):
        wait_bytes(hidden, 1, hidden_recv.at[r])
        block = hidden.at[at_chip(r)]
        to_exp(block, block, exp_send.at[4], hidden_recv.at[chips], sibling).start()
    wait_bytes(hidden, 1, hidden_recv.at[0])
    wait_bytes(hidden, chips - 1, hidden_recv.at[chips])

    tiles = [slice(i * LANES, (i + 1) * LANES) for i in range(cols // LANES)]
    per_part = n_exp // PARTS
    packet = per_dev * per_part

    def places(s, q_in_part):
        return pl.ds(s * per_part + q_in_part, n_ctx, stride=packet)

    def spread_rows(p, q_in_part, value):
        for s in range(per_dev):
            for i, lanes in enumerate(tiles):
                rows_f32.at[p * len(tiles) + i][places(s, q_in_part), :] = value[
                    s * n_ctx : (s + 1) * n_ctx, lanes
                ]

    def pack(ref, p):
        for i, lanes in enumerate(tiles):
            value = rows_f32[p * len(tiles) + i].reshape(n_ctx, packet, LANES)
            ref[p, :, :, lanes] = value.astype(bf16)

    def unpack(ref, p):
        for i, lanes in enumerate(tiles):
            value = ref[p, :, :, lanes].astype(f32)
            rows_f32[p * len(tiles) + i] = value.reshape(n_ctx * packet, LANES)

    def column_rows(s, p, q_in_part):
        return jnp.concatenate(
            [
                rows_f32.at[p * len(tiles) + i][places(s, q_in_part), :]
                for i in range(len(tiles))
            ],
            axis=1,
        ).astype(bf16)

    def exchange_part(src, dst, p, phase):
        exchange(src.at[p], dst.at[p], phase + p)
        dst[p, me_c] = src[p, me_c]

    send_own(2)
    pass_on_neighbours(1)
    pass_on_opposite(0)
    squares = jnp.zeros((token_count, cols), f32)
    for q in range(n_exp):
        h = hidden[q].astype(f32)
        squares = squares + h * h
    inverse = lax.rsqrt(jnp.sum(squares, axis=1, keepdims=True) / d_model + 1e-06)
    for q in range(n_exp):
        columns = slice(q * cols, (q + 1) * cols)
        value = hidden[q].astype(f32) * inverse * moe_gain_ref[:, columns]
        expert_in[:, columns] = value.astype(bf16)
        p, q_in_part = q // per_part, q % per_part
        spread_rows(p, q_in_part, dot(rows_of, expert_in[:, columns]))
        if q_in_part == per_part - 1:
            pack(rows_out, p)
            exchange_part(rows_out, rows_in, p, 2)

    logits = lax.dot_general(expert_in[...], router_ref[...], NT, preferred_element_type=f32)
    named_t, chosen_t = named.T, chosen.T
    score = 1.0 / (1.0 + jnp.exp(-logits))
    picked_score = score * named_t[:, 0:n_ctx]
    gate = picked_score / jnp.sum(picked_score, axis=1, keepdims=True)
    gate_rows = jnp.concatenate([gate] * per_dev, axis=1) * chosen_t
    gate_lead = leading(gate_rows)
    gate_high = gate_lead.astype(bf16)
    gate_low = (gate_rows - gate_lead).astype(bf16)
    pass_on_neighbours(2)
    pass_on_opposite(1)


    for p in range(PARTS):
        wait_bytes(rows_in.at[p], n_ctx - 1, ctx_recv.at[2 + p])
        unpack(rows_in, p)
        for q_in_part in range(per_part):
            first = (p * per_part + q_in_part) * cols
            for s in range(per_dev):
                tokens[s * n_ctx : (s + 1) * n_ctx, first : first + cols] = column_rows(
                    s, p, q_in_part
                )

    complete(0)
    complete(1)

    def hidden_units(first, count):
        units = pl.ds(first, count)
        g = lax.dot_general(tokens[...], w_gate[units, :], NT, preferred_element_type=f32)
        u = lax.dot_general(tokens[...], w_up[units, :], NT, preferred_element_type=f32)
        act[:, units] = (silu(g) * u).astype(bf16)

    chunk = min(256, ff_total)

    def units_step(i, carry):
        hidden_units(pl.multiple_of(i * chunk, chunk), chunk)
        return carry

    lax.fori_loop(0, ff_total // chunk, units_step, 0)
    if ff_total % chunk:
        hidden_units(ff_total // chunk * chunk, ff_total % chunk)

    pass_on_opposite(2)
    complete(2)

    for p in range(PARTS):

        def down_step(q_in_part, carry, p=p):
            first = (p * per_part + q_in_part) * cols
            columns = pl.ds(pl.multiple_of(first, cols), cols)
            spread_rows(p, q_in_part, dot(act[...], w_down[:, columns]))
            return carry

        lax.fori_loop(0, per_part, down_step, 0)
        pack(back_out, p)
        exchange_part(back_out, back_in, p, 4)

    def moe_columns(p, q_in_part):
        value = jnp.concatenate([column_rows(s, p, q_in_part) for s in range(per_dev)], axis=0)
        return dot(gate_high, value) + dot(gate_low, value)

    own_part, own_q = me_e // per_part, lax.rem(me_e, per_part)
    for p in range(PARTS):
        wait_bytes(back_in.at[p], n_ctx - 1, ctx_recv.at[4 + p])
        unpack(back_in, p)
        for away in range(per_part - 1, -1, -1):
            q_in_part = lax.rem(own_q + away, per_part)
            q = p * per_part + q_in_part

            def send_columns(q=q, p=p, q_in_part=q_in_part):
                moe_out[q] = moe_columns(p, q_in_part).astype(bf16)
                to_exp(moe_out.at[q], moe_in.at[me_e], exp_send.at[2], exp_recv.at[2], q).start()

            if away:
                send_columns()
            else:
                pl.when(own_part != p)(send_columns)
    total = moe_columns(own_part, own_q) + hidden[me_e].astype(f32)
    wait_bytes(moe_in, n_exp - 1, exp_recv.at[2])
    for d in range(1, n_exp):
        total = total + moe_in[exp_peer(d)].astype(f32)
    out_ref[...] = total.astype(bf16)

    wait_bytes(state_out, n_ctx - 1, ctx_send.at[0])
    wait_bytes(enter_out, n_ctx - 1, ctx_send.at[1])
    wait_bytes(decay_in, n_ctx - 1, ctx_send.at[6])
    for p in range(PARTS):
        wait_bytes(rows_out.at[p], n_ctx - 1, ctx_send.at[2 + p])
        wait_bytes(back_out.at[p], n_ctx - 1, ctx_send.at[4 + p])
    for phase, count in enumerate((chips, chips - 1, n_exp - 1, chips, chips - 1)):
        wait_bytes(mix_out, count, exp_send.at[phase])
    for i in range(3):
        for group, slots in enumerate((2, 1, 1, 2, 1)):
            wait_bytes(w_gate, slots * ff_part, w_send.at[i, group])


def per_device(n_ctx, n_exp, *args):
    (x, z, b, c, step, rate, norm_gain, out_w, stream, moe_gain, router, ids, wg, wu, wd) = args
    t, width = x.shape
    cols = stream.shape[1]
    d_model = cols * n_exp
    ff_part = wg.shape[1]
    ff_total = ff_part * n_exp
    part_rows = width // n_ctx
    stride = SLOTS // n_exp * n_exp
    row_count = n_ctx * (SLOTS // n_exp)
    vmem, dma = pltpu.VMEM, pltpu.SemaphoreType.DMA
    anywhere = pl.BlockSpec(memory_space=pl.ANY)
    rate, norm_gain, moe_gain = (v.reshape(1, -1) for v in (rate, norm_gain, moe_gain))
    router, ids = router.T, ids.T
    inputs = (x, z, b, c, step, rate, norm_gain, out_w, stream, moe_gain, router, ids)
    return pl.pallas_call(
        functools.partial(layer_kernel, n_ctx, n_exp),
        out_shape=jax.ShapeDtypeStruct((t, cols), bf16),
        in_specs=[anywhere] * 15,
        out_specs=pl.BlockSpec(memory_space=pltpu.VMEM),
        scratch_shapes=[
            *(vmem(v.shape, v.dtype) for v in inputs),
            vmem((ff_total, d_model), bf16),
            vmem((ff_total, d_model), bf16),
            vmem((ff_total, d_model), bf16),
            vmem((n_ctx, 2 * part_rows, N), bf16),
            vmem((n_ctx, 2 * part_rows, N), bf16),
            vmem((step.shape[0], 1, N), f32),
            vmem((n_ctx, 1, N), f32),
            vmem((n_ctx, part_rows, N), f32),
            vmem((n_ctx, part_rows, N), f32),
            vmem((t, width), f32),
            vmem((t, width), bf16),
            vmem((n_exp, t, cols), bf16),
            vmem((n_exp, t, cols), bf16),
            vmem((n_exp, t, cols), bf16),
            vmem((t, d_model), bf16),
            vmem((PARTS * cols // LANES, n_ctx * stride // PARTS, LANES), f32),
            vmem((PARTS, n_ctx, stride // PARTS, cols), bf16),
            vmem((PARTS, n_ctx, stride // PARTS, cols), bf16),
            vmem((row_count, d_model), bf16),
            vmem((row_count, ff_total), bf16),
            vmem((PARTS, n_ctx, stride // PARTS, cols), bf16),
            vmem((PARTS, n_ctx, stride // PARTS, cols), bf16),
            vmem((n_exp, t, cols), bf16),
            vmem((n_exp, t, cols), bf16),
            dma((15,)),
            dma((7,)),
            dma((7,)),
            dma((5,)),
            dma((3,)),
            dma((4,)),
            dma((5,)),
            dma((3, 5)),
            dma((3, 6)),
        ],
        compiler_params=pltpu.CompilerParams(
            collective_id=0, has_side_effects=True, vmem_limit_bytes=56 * 1024 * 1024
        ),
        name="layer",
    )(
        *inputs,
        wg[0],
        wu[0],
        wd[0],
    )


def solution(mesh):
    in_specs = (
        P("ctx", "exp"),
        P("ctx", "exp"),
        P("ctx", "exp"),
        P("ctx", "exp"),
        P("exp", "ctx"),
        P("exp"),
        P("exp"),
        P("exp", None),
        P("ctx", "exp"),
        P(),
        P(),
        P("ctx", None),
        P("ctx", "exp", None),
        P("ctx", "exp", None),
        P("ctx", "exp", None),
    )
    return jax.shard_map(
        functools.partial(per_device, mesh.shape["ctx"], mesh.shape["exp"]),
        mesh=mesh,
        in_specs=in_specs,
        out_specs=P("ctx", "exp"),
        check_vma=False,
    )
```

```python
import functools

import jax
import jax.numpy as jnp
from jax import lax
from jax.experimental import pallas as pl
from jax.experimental.pallas import tpu as pltpu
from jax.sharding import PartitionSpec as P

P_SIZE = 64
N = 128
LANES = 128
SLOTS = 16
PARTS = 2
CORES = 2
MESH = pl.DeviceIdType.MESH
NT = (((1,), (1,)), ((), ()))
f32 = jnp.float32
bf16 = jnp.bfloat16


def iota(shape, dim):
    return lax.broadcasted_iota(jnp.int32, shape, dim)


def dot(a, b):
    return jnp.dot(a, b, preferred_element_type=f32)


def silu(v):
    return v / (1.0 + jnp.exp(-v))


def leading(v):
    scaled = v * 65537.0
    return scaled - (scaled - v)


def wait_bytes(ref, count, sem):
    view = ref.at[pl.ds(0, count)]
    pltpu.make_async_copy(view, view, sem).wait()


def layer_kernel(
    n_ctx,
    n_exp,
    x_hbm,
    z_hbm,
    b_hbm,
    c_hbm,
    step_hbm,
    rate_hbm,
    norm_gain_hbm,
    out_w_hbm,
    stream_hbm,
    moe_gain_hbm,
    router_hbm,
    ids_hbm,
    w_gate_hbm,
    w_up_hbm,
    w_down_hbm,
    out_ref,
    x_ref,
    z_ref,
    b_ref,
    c_ref,
    step_ref,
    rate_ref,
    norm_gain_ref,
    out_w,
    stream_ref,
    moe_gain_ref,
    router_ref,
    ids_ref,
    w_gate,
    w_up,
    w_down,
    state_out,
    state_in,
    decay_out,
    decay_in,
    enter_out,
    enter_in,
    inner,
    mixed,
    mix_out,
    mix_in,
    hidden,
    expert_in,
    rows_f32,
    rows_out,
    rows_in,
    tokens,
    act,
    back_out,
    back_in,
    moe_out,
    moe_in,
    local_sem,
    ctx_send,
    ctx_recv,
    exp_send,
    exp_recv,
    pair_recv,
    hidden_recv,
    w_send,
    w_recv,
):
    me_c, me_e = lax.axis_index("ctx"), lax.axis_index("exp")
    token_count, width = x_ref.shape
    head_count = step_ref.shape[0]
    pair_count = width // LANES
    part_rows = width // n_ctx
    cols = stream_ref.shape[1]
    d_model = cols * n_exp
    ff_part = w_gate_hbm.shape[0]
    ff_total = ff_part * n_exp
    per_dev = SLOTS // n_exp
    row_count = n_ctx * per_dev

    def ctx_peer(d):
        back = n_ctx - d
        odd, away = lax.rem(back, 2), (back + 1) // 2
        return lax.rem(me_c + odd * away + (1 - odd) * (n_ctx - away), n_ctx)


    def exp_peer(d):
        return lax.rem(me_e + d, n_exp)

    def to_exp(src, dst, send, recv, peer):
        return pltpu.make_async_remote_copy(
            src_ref=src,
            dst_ref=dst,
            send_sem=send,
            recv_sem=recv,
            device_id=(me_c, peer),
            device_id_type=MESH,
        )

    def exchange(src, dst, phase, entry=lambda peer: peer):
        def one(d, carry):
            peer = ctx_peer(d)
            pltpu.make_async_remote_copy(
                src_ref=src.at[entry(peer)],
                dst_ref=dst.at[me_c],
                send_sem=ctx_send.at[phase],
                recv_sem=ctx_recv.at[phase],
                device_id=(peer, me_e),
                device_id_type=MESH,
            ).start()
            return carry

        lax.fori_loop(1, n_ctx, one, 0, unroll=9 if n_ctx % 9 == 1 else 1)

    barrier = pltpu.get_barrier_semaphore()

    def greet_ctx(d, carry):
        pl.semaphore_signal(barrier, inc=1, device_id=(ctx_peer(d), me_e), device_id_type=MESH)
        return carry

    def greet_exp(d, carry):
        pl.semaphore_signal(barrier, inc=1, device_id=(me_c, exp_peer(d)), device_id_type=MESH)
        return carry

    lax.fori_loop(1, n_ctx, greet_ctx, 0)
    lax.fori_loop(1, n_exp, greet_exp, 0)

    fetched = [
        pltpu.make_async_copy(hbm, vmem, local_sem.at[3 + i])
        for i, (hbm, vmem) in enumerate(
            (
                (step_hbm, step_ref),
                (rate_hbm, rate_ref),
                (x_hbm, x_ref),
                (b_hbm, b_ref),
                (c_hbm, c_ref),
                (z_hbm, z_ref),
                (ids_hbm, ids_ref),
                (norm_gain_hbm, norm_gain_ref),
                (stream_hbm, stream_ref),
                (moe_gain_hbm, moe_gain_ref),
                (router_hbm, router_ref),
                (out_w_hbm, out_w),
            )
        )
    ]
    for copy in fetched:
        copy.start()
    weights = ((w_gate_hbm, w_gate), (w_up_hbm, w_up), (w_down_hbm, w_down))

    def part(ref, index, first=0, rows=ff_part):
        return ref.at[pl.ds(pl.multiple_of(index * ff_part + first, 16), rows)]

    own_copies = [
        pltpu.make_async_copy(hbm, part(buf, me_e), local_sem.at[i])
        for i, (hbm, buf) in enumerate(weights)
    ]
    for copy in own_copies:
        copy.start()

    for copy in fetched[0:4]:
        copy.wait()
    step = step_ref[...]
    diagonal = iota((head_count, head_count), 0) == iota((head_count, head_count), 1)
    rate = jnp.sum(jnp.where(diagonal, rate_ref[...], 0.0), axis=1, keepdims=True)
    lane_t = iota((head_count, token_count), 1)
    running = -(step * rate)
    shift = 1
    while shift < token_count:
        running = running + jnp.where(lane_t >= shift, pltpu.roll(running, shift, 1), 0.0)
        shift *= 2
    stacked = jnp.concatenate(
        [running, step, jnp.zeros((token_count - 2 * head_count, token_count), f32)], axis=0
    )
    by_token = stacked.T
    run_t = by_token[:, 0:head_count]
    step_t = by_token[:, head_count : 2 * head_count]
    last = run_t[token_count - 1 : token_count, :]
    tail = jnp.exp(last - run_t)
    grown = jnp.exp(run_t)
    total_decay = jnp.exp(last)
    for h in range(head_count):
        decay_out[h] = jnp.broadcast_to(total_decay[:, h : h + 1], (1, N))

    first_half = iota((token_count, LANES), 1) < P_SIZE

    def expand(per_head, k):
        return jnp.where(
            first_half, per_head[:, 2 * k : 2 * k + 1], per_head[:, 2 * k + 1 : 2 * k + 2]
        )

    b_block = b_ref[...]
    weighted = []
    for k in range(pair_count):
        lanes = slice(k * LANES, (k + 1) * LANES)
        stepped = (expand(step_t, k) * x_ref[:, lanes].astype(f32)).astype(bf16)
        weighted.append(stepped)
        carried = (expand(tail, k) * stepped.astype(f32)).T.astype(bf16)
        state = dot(carried, b_block)
        for i in range(LANES // part_rows):
            j = k * LANES // part_rows + i
            piece = state[i * part_rows : (i + 1) * part_rows, :]
            lead = leading(piece)
            state_out[j] = jnp.concatenate([lead, piece - lead], axis=0).astype(bf16)

    pl.semaphore_wait(barrier, n_ctx - 1 + n_exp - 1)

    exchange(state_out, state_in, 0)
    exchange(decay_out, decay_in, 6, lambda peer: peer * part_rows // P_SIZE)

    chips = n_exp // CORES
    me_x, core = me_e // CORES, lax.rem(me_e, CORES)

    def at_chip(d):
        return lax.rem(me_x + d, chips) * CORES + core

    right, left, opposite = at_chip(1), at_chip(chips - 1), at_chip(2)
    sibling = me_x * CORES + 1 - core
    half = ff_part // 32 * 16

    def send_part(i, index, first, rows, group, arrival, peer, hbm=None):
        buf = weights[i][1]
        to_exp(
            part(buf, index, first, rows) if hbm is None else hbm,
            part(buf, index, first, rows),
            w_send.at[i, group],
            w_recv.at[i, arrival],
            peer,
        ).start()

    def arrived(i, arrival, slots):
        wait_bytes(w_gate, slots * ff_part, w_recv.at[i, arrival])

    def send_own(i):
        hbm = weights[i][0]
        send_part(i, me_e, 0, ff_part, 0, 0, right, hbm)
        send_part(i, me_e, 0, ff_part, 0, 1, left, hbm)
        send_part(i, me_e, 0, ff_part, 1, 3, sibling, hbm)

    def pass_on_neighbours(i):
        arrived(i, 0, 1)
        arrived(i, 1, 1)
        send_part(i, left, 0, half, 2, 2, right)
        send_part(i, right, half, ff_part - half, 2, 2, left)
        send_part(i, left, 0, ff_part, 3, 4, sibling)
        send_part(i, right, 0, ff_part, 3, 4, sibling)

    def pass_on_opposite(i):
        arrived(i, 2, 1)
        send_part(i, opposite, 0, ff_part, 4, 5, sibling)

    def complete(i):
        own_copies[i].wait()
        arrived(i, 3, 1)
        arrived(i, 4, 2)
        arrived(i, 5, 1)

    send_own(0)
    send_own(1)

    fetched[4].wait()
    c_block = c_ref[...]
    scores = lax.dot_general(c_block, b_block, NT, preferred_element_type=f32)
    lower = iota((token_count, token_count), 0) >= iota((token_count, token_count), 1)

    def mix_head(h, values):
        spread = run_t[:, h : h + 1] - running[h : h + 1, :]
        decay = jnp.where(lower, jnp.exp(jnp.where(lower, spread, 0.0)), 0.0)
        return dot((decay * scores).astype(bf16), values)

    for k in range(pair_count):
        inner[:, k * LANES : (k + 1) * LANES] = jnp.where(
            first_half, mix_head(2 * k, weighted[k]), mix_head(2 * k + 1, weighted[k])
        )

    state_in[me_c] = state_out[me_c]
    decay_in[me_c] = decay_out[me_c * part_rows // P_SIZE]
    wait_bytes(state_in, n_ctx - 1, ctx_recv.at[0])
    wait_bytes(decay_in, n_ctx - 1, ctx_recv.at[6])

    def chain(i, entering):
        enter_out[i] = entering
        block = state_in[i].astype(f32)
        r = part_rows
        return decay_in[i] * entering + (block[0:r] + block[r : 2 * r])

    lax.fori_loop(0, n_ctx, chain, jnp.zeros((part_rows, N), f32), unroll=min(8, n_ctx))
    exchange(enter_out, enter_in, 1)
    enter_in[me_c] = enter_out[me_c]

    for copy in fetched[5:]:
        copy.wait()
    row_r = iota((row_count, token_count), 0)
    expert_of, slot_of = lax.rem(row_r, n_ctx), row_r // n_ctx
    named = jnp.zeros((row_count, token_count), f32)
    for k in range(ids_ref.shape[0]):
        named = named + jnp.where(ids_ref[k : k + 1, :] == expert_of, 1.0, 0.0)
    earlier = iota((token_count, token_count), 0) < iota((token_count, token_count), 1)
    rank = dot(named.astype(bf16), jnp.where(earlier, 1.0, 0.0).astype(bf16))
    wanted = (slot_of + me_e * per_dev).astype(f32)
    chosen = jnp.where(rank == wanted, named, 0.0)
    rows_of = chosen.astype(bf16)
    gating = [silu(z_ref[:, k * LANES : (k + 1) * LANES].astype(f32)) for k in range(pair_count)]

    pass_on_neighbours(0)

    wait_bytes(enter_in, n_ctx - 1, ctx_recv.at[1])
    entering = enter_in[...].reshape(width, N)
    lead = leading(entering)
    carried_in = lax.dot_general(
        c_block, lead.astype(bf16), NT, preferred_element_type=f32
    ) + lax.dot_general(
        c_block, (entering - lead).astype(bf16), NT, preferred_element_type=f32
    )
    gated = []
    for k in range(pair_count):
        lanes = slice(k * LANES, (k + 1) * LANES)
        ssd_out = inner[:, lanes] + expand(grown, k) * carried_in[:, lanes]
        gated.append(ssd_out * gating[k])
    squares = gated[0] * gated[0]
    for g in gated[1:]:
        squares = squares + g * g
    inverse = lax.rsqrt(jnp.sum(squares, axis=1, keepdims=True) / width + 1e-05)
    for k in range(pair_count):
        lanes = slice(k * LANES, (k + 1) * LANES)
        mixed[:, lanes] = (gated[k] * inverse * norm_gain_ref[:, lanes]).astype(bf16)

    def out_columns(q):
        return dot(mixed[...], out_w[:, pl.ds(pl.multiple_of(q * cols, cols), cols)])

    away = (2, 1, 3)
    for r in (*away, 0):
        chip = lax.rem(me_x + r, chips)
        mix_out[r] = out_columns(chip * CORES + 1 - core).astype(bf16)
        to_exp(mix_out.at[r], mix_in.at[r], exp_send.at[0], pair_recv.at[r], sibling).start()

    def pair_columns(r):
        value = out_columns(at_chip(r))
        wait_bytes(mix_in, 1, pair_recv.at[r])
        return value + mix_in[r].astype(f32)

    for r in away:
        mix_out[chips + r] = pair_columns(r).astype(bf16)
        to_exp(
            mix_out.at[chips + r],
            mix_in.at[2 * chips - r],
            exp_send.at[1],
            exp_recv.at[0],
            at_chip(r),
        ).start()
    own = pair_columns(0) + stream_ref[...].astype(f32)
    wait_bytes(mix_in, chips - 1, exp_recv.at[0])
    for r in away:
        own = own + mix_in[chips + r].astype(f32)

    hidden[me_e] = own.astype(bf16)
    mine = hidden.at[me_e]
    for r in away:
        to_exp(mine, mine, exp_send.at[3], hidden_recv.at[chips - r], at_chip(r)).start()
    to_exp(mine, mine, exp_send.at[3], hidden_recv.at[0], sibling).start()
    for r in (1, 3, 2):
        wait_bytes(hidden, 1, hidden_recv.at[r])
        block = hidden.at[at_chip(r)]
        to_exp(block, block, exp_send.at[4], hidden_recv.at[chips], sibling).start()
    wait_bytes(hidden, 1, hidden_recv.at[0])
    wait_bytes(hidden, chips - 1, hidden_recv.at[chips])

    tiles = [slice(i * LANES, (i + 1) * LANES) for i in range(cols // LANES)]
    per_part = n_exp // PARTS
    packet = per_dev * per_part

    def places(s, q_in_part):
        return pl.ds(s * per_part + q_in_part, n_ctx, stride=packet)

    def spread_rows(p, q_in_part, value):
        for s in range(per_dev):
            for i, lanes in enumerate(tiles):
                rows_f32.at[p * len(tiles) + i][places(s, q_in_part), :] = value[
                    s * n_ctx : (s + 1) * n_ctx, lanes
                ]

    def pack(ref, p):
        for i, lanes in enumerate(tiles):
            value = rows_f32[p * len(tiles) + i].reshape(n_ctx, packet, LANES)
            ref[p, :, :, lanes] = value.astype(bf16)

    def unpack(ref, p):
        for i, lanes in enumerate(tiles):
            value = ref[p, :, :, lanes].astype(f32)
            rows_f32[p * len(tiles) + i] = value.reshape(n_ctx * packet, LANES)

    def column_rows(s, p, q_in_part):
        return jnp.concatenate(
            [
                rows_f32.at[p * len(tiles) + i][places(s, q_in_part), :]
                for i in range(len(tiles))
            ],
            axis=1,
        ).astype(bf16)

    def exchange_part(src, dst, p, phase):
        exchange(src.at[p], dst.at[p], phase + p)
        dst[p, me_c] = src[p, me_c]

    send_own(2)
    pass_on_neighbours(1)
    pass_on_opposite(0)
    squares = jnp.zeros((token_count, cols), f32)
    for q in range(n_exp):
        h = hidden[q].astype(f32)
        squares = squares + h * h
    inverse = lax.rsqrt(jnp.sum(squares, axis=1, keepdims=True) / d_model + 1e-06)
    for q in range(n_exp):
        columns = slice(q * cols, (q + 1) * cols)
        value = hidden[q].astype(f32) * inverse * moe_gain_ref[:, columns]
        expert_in[:, columns] = value.astype(bf16)
        p, q_in_part = q // per_part, q % per_part
        spread_rows(p, q_in_part, dot(rows_of, expert_in[:, columns]))
        if q_in_part == per_part - 1:
            pack(rows_out, p)
            exchange_part(rows_out, rows_in, p, 2)

    logits = lax.dot_general(expert_in[...], router_ref[...], NT, preferred_element_type=f32)
    named_t, chosen_t = named.T, chosen.T
    score = 1.0 / (1.0 + jnp.exp(-logits))
    picked_score = score * named_t[:, 0:n_ctx]
    gate = picked_score / jnp.sum(picked_score, axis=1, keepdims=True)
    gate_rows = jnp.concatenate([gate] * per_dev, axis=1) * chosen_t
    gate_lead = leading(gate_rows)
    gate_high = gate_lead.astype(bf16)
    gate_low = (gate_rows - gate_lead).astype(bf16)
    pass_on_neighbours(2)
    pass_on_opposite(1)


    for p in range(PARTS):
        wait_bytes(rows_in.at[p], n_ctx - 1, ctx_recv.at[2 + p])
        unpack(rows_in, p)
        for q_in_part in range(per_part):
            first = (p * per_part + q_in_part) * cols
            for s in range(per_dev):
                tokens[s * n_ctx : (s + 1) * n_ctx, first : first + cols] = column_rows(
                    s, p, q_in_part
                )

    complete(0)
    complete(1)

    def hidden_units(first, count):
        units = pl.ds(first, count)
        g = lax.dot_general(tokens[...], w_gate[units, :], NT, preferred_element_type=f32)
        u = lax.dot_general(tokens[...], w_up[units, :], NT, preferred_element_type=f32)
        act[:, units] = (silu(g) * u).astype(bf16)

    chunk = min(256, ff_total)

    def units_step(i, carry):
        hidden_units(pl.multiple_of(i * chunk, chunk), chunk)
        return carry

    lax.fori_loop(0, ff_total // chunk, units_step, 0)
    if ff_total % chunk:
        hidden_units(ff_total // chunk * chunk, ff_total % chunk)

    pass_on_opposite(2)
    complete(2)

    for p in range(PARTS):

        def down_step(q_in_part, carry, p=p):
            first = (p * per_part + q_in_part) * cols
            columns = pl.ds(pl.multiple_of(first, cols), cols)
            spread_rows(p, q_in_part, dot(act[...], w_down[:, columns]))
            return carry

        lax.fori_loop(0, per_part, down_step, 0)
        pack(back_out, p)
        exchange_part(back_out, back_in, p, 4)

    def moe_columns(p, q_in_part):
        value = jnp.concatenate([column_rows(s, p, q_in_part) for s in range(per_dev)], axis=0)
        return dot(gate_high, value) + dot(gate_low, value)

    own_part, own_q = me_e // per_part, lax.rem(me_e, per_part)
    for p in range(PARTS):
        wait_bytes(back_in.at[p], n_ctx - 1, ctx_recv.at[4 + p])
        unpack(back_in, p)
        for away in range(per_part - 1, -1, -1):
            q_in_part = lax.rem(own_q + away, per_part)
            q = p * per_part + q_in_part

            def send_columns(q=q, p=p, q_in_part=q_in_part):
                moe_out[q] = moe_columns(p, q_in_part).astype(bf16)
                to_exp(moe_out.at[q], moe_in.at[me_e], exp_send.at[2], exp_recv.at[2], q).start()

            if away:
                send_columns()
            else:
                pl.when(own_part != p)(send_columns)
    total = moe_columns(own_part, own_q) + hidden[me_e].astype(f32)
    wait_bytes(moe_in, n_exp - 1, exp_recv.at[2])
    for d in range(1, n_exp):
        total = total + moe_in[exp_peer(d)].astype(f32)
    out_ref[...] = total.astype(bf16)

    wait_bytes(state_out, n_ctx - 1, ctx_send.at[0])
    wait_bytes(enter_out, n_ctx - 1, ctx_send.at[1])
    wait_bytes(decay_in, n_ctx - 1, ctx_send.at[6])
    for p in range(PARTS):
        wait_bytes(rows_out.at[p], n_ctx - 1, ctx_send.at[2 + p])
        wait_bytes(back_out.at[p], n_ctx - 1, ctx_send.at[4 + p])
    for phase, count in enumerate((chips, chips - 1, n_exp - 1, chips, chips - 1)):
        wait_bytes(mix_out, count, exp_send.at[phase])
    for i in range(3):
        for group, slots in enumerate((2, 1, 1, 2, 1)):
            wait_bytes(w_gate, slots * ff_part, w_send.at[i, group])


def per_device(n_ctx, n_exp, *args):
    (x, z, b, c, step, rate, norm_gain, out_w, stream, moe_gain, router, ids, wg, wu, wd) = args
    t, width = x.shape
    cols = stream.shape[1]
    d_model = cols * n_exp
    ff_part = wg.shape[1]
    ff_total = ff_part * n_exp
    part_rows = width // n_ctx
    stride = SLOTS // n_exp * n_exp
    row_count = n_ctx * (SLOTS // n_exp)
    vmem, dma = pltpu.VMEM, pltpu.SemaphoreType.DMA
    anywhere = pl.BlockSpec(memory_space=pl.ANY)
    rate, norm_gain, moe_gain = (v.reshape(1, -1) for v in (rate, norm_gain, moe_gain))
    router, ids = router.T, ids.T
    inputs = (x, z, b, c, step, rate, norm_gain, out_w, stream, moe_gain, router, ids)
    return pl.pallas_call(
        functools.partial(layer_kernel, n_ctx, n_exp),
        out_shape=jax.ShapeDtypeStruct((t, cols), bf16),
        in_specs=[anywhere] * 15,
        out_specs=pl.BlockSpec(memory_space=pltpu.VMEM),
        scratch_shapes=[
            *(vmem(v.shape, v.dtype) for v in inputs),
            vmem((ff_total, d_model), bf16),
            vmem((ff_total, d_model), bf16),
            vmem((ff_total, d_model), bf16),
            vmem((n_ctx, 2 * part_rows, N), bf16),
            vmem((n_ctx, 2 * part_rows, N), bf16),
            vmem((step.shape[0], 1, N), f32),
            vmem((n_ctx, 1, N), f32),
            vmem((n_ctx, part_rows, N), f32),
            vmem((n_ctx, part_rows, N), f32),
            vmem((t, width), f32),
            vmem((t, width), bf16),
            vmem((n_exp, t, cols), bf16),
            vmem((n_exp, t, cols), bf16),
            vmem((n_exp, t, cols), bf16),
            vmem((t, d_model), bf16),
            vmem((PARTS * cols // LANES, n_ctx * stride // PARTS, LANES), f32),
            vmem((PARTS, n_ctx, stride // PARTS, cols), bf16),
            vmem((PARTS, n_ctx, stride // PARTS, cols), bf16),
            vmem((row_count, d_model), bf16),
            vmem((row_count, ff_total), bf16),
            vmem((PARTS, n_ctx, stride // PARTS, cols), bf16),
            vmem((PARTS, n_ctx, stride // PARTS, cols), bf16),
            vmem((n_exp, t, cols), bf16),
            vmem((n_exp, t, cols), bf16),
            dma((15,)),
            dma((7,)),
            dma((7,)),
            dma((5,)),
            dma((3,)),
            dma((4,)),
            dma((5,)),
            dma((3, 5)),
            dma((3, 6)),
        ],
        compiler_params=pltpu.CompilerParams(
            collective_id=0, has_side_effects=True, vmem_limit_bytes=56 * 1024 * 1024
        ),
        name="layer",
    )(
        *inputs,
        wg[0],
        wu[0],
        wd[0],
    )


def solution(mesh):
    in_specs = (
        P("ctx", "exp"),
        P("ctx", "exp"),
        P("ctx", "exp"),
        P("ctx", "exp"),
        P("exp", "ctx"),
        P("exp"),
        P("exp"),
        P("exp", None),
        P("ctx", "exp"),
        P(),
        P(),
        P("ctx", None),
        P("ctx", "exp", None),
        P("ctx", "exp", None),
        P("ctx", "exp", None),
    )
    return jax.shard_map(
        functools.partial(per_device, mesh.shape["ctx"], mesh.shape["exp"]),
        mesh=mesh,
        in_specs=in_specs,
        out_specs=P("ctx", "exp"),
        check_vma=False,
    )
```

```python
import functools

import jax
import jax.numpy as jnp
from jax import lax
from jax.experimental import pallas as pl
from jax.experimental.pallas import tpu as pltpu
from jax.sharding import PartitionSpec as P

P_SIZE = 64
N = 128
LANES = 128
SLOTS = 16
PARTS = 2
CORES = 2
MESH = pl.DeviceIdType.MESH
NT = (((1,), (1,)), ((), ()))
f32 = jnp.float32
bf16 = jnp.bfloat16


def iota(shape, dim):
    return lax.broadcasted_iota(jnp.int32, shape, dim)


def dot(a, b):
    return jnp.dot(a, b, preferred_element_type=f32)


def silu(v):
    return v / (1.0 + jnp.exp(-v))


def leading(v):
    scaled = v * 65537.0
    return scaled - (scaled - v)


def wait_bytes(ref, count, sem):
    view = ref.at[pl.ds(0, count)]
    pltpu.make_async_copy(view, view, sem).wait()


def layer_kernel(
    n_ctx,
    n_exp,
    x_hbm,
    z_hbm,
    b_hbm,
    c_hbm,
    step_hbm,
    rate_hbm,
    norm_gain_hbm,
    out_w_hbm,
    stream_hbm,
    moe_gain_hbm,
    router_hbm,
    ids_hbm,
    w_gate_hbm,
    w_up_hbm,
    w_down_hbm,
    out_ref,
    x_ref,
    z_ref,
    b_ref,
    c_ref,
    step_ref,
    rate_ref,
    norm_gain_ref,
    out_w,
    stream_ref,
    moe_gain_ref,
    router_ref,
    ids_ref,
    w_gate,
    w_up,
    w_down,
    state_out,
    state_in,
    decay_out,
    decay_in,
    enter_out,
    enter_in,
    inner,
    mixed,
    mix_out,
    mix_in,
    hidden,
    expert_in,
    rows_f32,
    rows_out,
    rows_in,
    tokens,
    act,
    back_out,
    back_in,
    moe_out,
    moe_in,
    local_sem,
    ctx_send,
    ctx_recv,
    exp_send,
    exp_recv,
    pair_recv,
    hidden_recv,
    w_send,
    w_recv,
):
    me_c, me_e = lax.axis_index("ctx"), lax.axis_index("exp")
    token_count, width = x_ref.shape
    head_count = step_ref.shape[0]
    pair_count = width // LANES
    part_rows = width // n_ctx
    cols = stream_ref.shape[1]
    d_model = cols * n_exp
    ff_part = w_gate_hbm.shape[0]
    ff_total = ff_part * n_exp
    per_dev = SLOTS // n_exp
    row_count = n_ctx * per_dev

    def ctx_peer(d):
        back = n_ctx - d
        odd, away = lax.rem(back, 2), (back + 1) // 2
        return lax.rem(me_c + odd * away + (1 - odd) * (n_ctx - away), n_ctx)


    def exp_peer(d):
        return lax.rem(me_e + d, n_exp)

    def to_exp(src, dst, send, recv, peer):
        return pltpu.make_async_remote_copy(
            src_ref=src,
            dst_ref=dst,
            send_sem=send,
            recv_sem=recv,
            device_id=(me_c, peer),
            device_id_type=MESH,
        )

    def exchange(src, dst, phase, entry=lambda peer: peer):
        def one(d, carry):
            peer = ctx_peer(d)
            pltpu.make_async_remote_copy(
                src_ref=src.at[entry(peer)],
                dst_ref=dst.at[me_c],
                send_sem=ctx_send.at[phase],
                recv_sem=ctx_recv.at[phase],
                device_id=(peer, me_e),
                device_id_type=MESH,
            ).start()
            return carry

        lax.fori_loop(1, n_ctx, one, 0, unroll=9 if n_ctx % 9 == 1 else 1)

    barrier = pltpu.get_barrier_semaphore()

    def greet_ctx(d, carry):
        pl.semaphore_signal(barrier, inc=1, device_id=(ctx_peer(d), me_e), device_id_type=MESH)
        return carry

    def greet_exp(d, carry):
        pl.semaphore_signal(barrier, inc=1, device_id=(me_c, exp_peer(d)), device_id_type=MESH)
        return carry

    lax.fori_loop(1, n_ctx, greet_ctx, 0)
    lax.fori_loop(1, n_exp, greet_exp, 0)

    fetched = [
        pltpu.make_async_copy(hbm, vmem, local_sem.at[3 + i])
        for i, (hbm, vmem) in enumerate(
            (
                (step_hbm, step_ref),
                (rate_hbm, rate_ref),
                (x_hbm, x_ref),
                (b_hbm, b_ref),
                (c_hbm, c_ref),
                (z_hbm, z_ref),
                (ids_hbm, ids_ref),
                (norm_gain_hbm, norm_gain_ref),
                (stream_hbm, stream_ref),
                (moe_gain_hbm, moe_gain_ref),
                (router_hbm, router_ref),
                (out_w_hbm, out_w),
            )
        )
    ]
    for copy in fetched:
        copy.start()
    weights = ((w_gate_hbm, w_gate), (w_up_hbm, w_up), (w_down_hbm, w_down))

    def part(ref, index, first=0, rows=ff_part):
        return ref.at[pl.ds(pl.multiple_of(index * ff_part + first, 16), rows)]

    own_copies = [
        pltpu.make_async_copy(hbm, part(buf, me_e), local_sem.at[i])
        for i, (hbm, buf) in enumerate(weights)
    ]
    for copy in own_copies:
        copy.start()

    for copy in fetched[0:4]:
        copy.wait()
    step = step_ref[...]
    diagonal = iota((head_count, head_count), 0) == iota((head_count, head_count), 1)
    rate = jnp.sum(jnp.where(diagonal, rate_ref[...], 0.0), axis=1, keepdims=True)
    lane_t = iota((head_count, token_count), 1)
    running = -(step * rate)
    shift = 1
    while shift < token_count:
        running = running + jnp.where(lane_t >= shift, pltpu.roll(running, shift, 1), 0.0)
        shift *= 2
    stacked = jnp.concatenate(
        [running, step, jnp.zeros((token_count - 2 * head_count, token_count), f32)], axis=0
    )
    by_token = stacked.T
    run_t = by_token[:, 0:head_count]
    step_t = by_token[:, head_count : 2 * head_count]
    last = run_t[token_count - 1 : token_count, :]
    tail = jnp.exp(last - run_t)
    grown = jnp.exp(run_t)
    total_decay = jnp.exp(last)
    for h in range(head_count):
        decay_out[h] = jnp.broadcast_to(total_decay[:, h : h + 1], (1, N))

    first_half = iota((token_count, LANES), 1) < P_SIZE

    def expand(per_head, k):
        return jnp.where(
            first_half, per_head[:, 2 * k : 2 * k + 1], per_head[:, 2 * k + 1 : 2 * k + 2]
        )

    b_block = b_ref[...]
    weighted = []
    for k in range(pair_count):
        lanes = slice(k * LANES, (k + 1) * LANES)
        stepped = (expand(step_t, k) * x_ref[:, lanes].astype(f32)).astype(bf16)
        weighted.append(stepped)
        carried = (expand(tail, k) * stepped.astype(f32)).T.astype(bf16)
        state = dot(carried, b_block)
        for i in range(LANES // part_rows):
            j = k * LANES // part_rows + i
            piece = state[i * part_rows : (i + 1) * part_rows, :]
            lead = leading(piece)
            state_out[j] = jnp.concatenate([lead, piece - lead], axis=0).astype(bf16)

    pl.semaphore_wait(barrier, n_ctx - 1 + n_exp - 1)

    exchange(state_out, state_in, 0)
    exchange(decay_out, decay_in, 6, lambda peer: peer * part_rows // P_SIZE)

    chips = n_exp // CORES
    me_x, core = me_e // CORES, lax.rem(me_e, CORES)

    def at_chip(d):
        return lax.rem(me_x + d, chips) * CORES + core

    right, left, opposite = at_chip(1), at_chip(chips - 1), at_chip(2)
    sibling = me_x * CORES + 1 - core
    half = ff_part // 32 * 16

    def send_part(i, index, first, rows, group, arrival, peer, hbm=None):
        buf = weights[i][1]
        to_exp(
            part(buf, index, first, rows) if hbm is None else hbm,
            part(buf, index, first, rows),
            w_send.at[i, group],
            w_recv.at[i, arrival],
            peer,
        ).start()

    def arrived(i, arrival, slots):
        wait_bytes(w_gate, slots * ff_part, w_recv.at[i, arrival])

    def send_own(i):
        hbm = weights[i][0]
        send_part(i, me_e, 0, ff_part, 0, 0, right, hbm)
        send_part(i, me_e, 0, ff_part, 0, 1, left, hbm)
        send_part(i, me_e, 0, ff_part, 1, 3, sibling, hbm)

    def pass_on_neighbours(i):
        arrived(i, 0, 1)
        arrived(i, 1, 1)
        send_part(i, left, 0, half, 2, 2, right)
        send_part(i, right, half, ff_part - half, 2, 2, left)
        send_part(i, left, 0, ff_part, 3, 4, sibling)
        send_part(i, right, 0, ff_part, 3, 4, sibling)

    def pass_on_opposite(i):
        arrived(i, 2, 1)
        send_part(i, opposite, 0, ff_part, 4, 5, sibling)

    def complete(i):
        own_copies[i].wait()
        arrived(i, 3, 1)
        arrived(i, 4, 2)
        arrived(i, 5, 1)

    send_own(0)
    send_own(1)

    fetched[4].wait()
    c_block = c_ref[...]
    scores = lax.dot_general(c_block, b_block, NT, preferred_element_type=f32)
    lower = iota((token_count, token_count), 0) >= iota((token_count, token_count), 1)

    def mix_head(h, values):
        spread = run_t[:, h : h + 1] - running[h : h + 1, :]
        decay = jnp.where(lower, jnp.exp(jnp.where(lower, spread, 0.0)), 0.0)
        return dot((decay * scores).astype(bf16), values)

    for k in range(pair_count):
        inner[:, k * LANES : (k + 1) * LANES] = jnp.where(
            first_half, mix_head(2 * k, weighted[k]), mix_head(2 * k + 1, weighted[k])
        )

    state_in[me_c] = state_out[me_c]
    decay_in[me_c] = decay_out[me_c * part_rows // P_SIZE]
    wait_bytes(state_in, n_ctx - 1, ctx_recv.at[0])
    wait_bytes(decay_in, n_ctx - 1, ctx_recv.at[6])

    def chain(i, entering):
        enter_out[i] = entering
        block = state_in[i].astype(f32)
        r = part_rows
        return decay_in[i] * entering + (block[0:r] + block[r : 2 * r])

    lax.fori_loop(0, n_ctx, chain, jnp.zeros((part_rows, N), f32), unroll=min(8, n_ctx))
    exchange(enter_out, enter_in, 1)
    enter_in[me_c] = enter_out[me_c]

    for copy in fetched[5:]:
        copy.wait()
    row_r = iota((row_count, token_count), 0)
    expert_of, slot_of = lax.rem(row_r, n_ctx), row_r // n_ctx
    named = jnp.zeros((row_count, token_count), f32)
    for k in range(ids_ref.shape[0]):
        named = named + jnp.where(ids_ref[k : k + 1, :] == expert_of, 1.0, 0.0)
    earlier = iota((token_count, token_count), 0) < iota((token_count, token_count), 1)
    rank = dot(named.astype(bf16), jnp.where(earlier, 1.0, 0.0).astype(bf16))
    wanted = (slot_of + me_e * per_dev).astype(f32)
    chosen = jnp.where(rank == wanted, named, 0.0)
    rows_of = chosen.astype(bf16)
    gating = [silu(z_ref[:, k * LANES : (k + 1) * LANES].astype(f32)) for k in range(pair_count)]

    pass_on_neighbours(0)

    wait_bytes(enter_in, n_ctx - 1, ctx_recv.at[1])
    entering = enter_in[...].reshape(width, N)
    lead = leading(entering)
    carried_in = lax.dot_general(
        c_block, lead.astype(bf16), NT, preferred_element_type=f32
    ) + lax.dot_general(
        c_block, (entering - lead).astype(bf16), NT, preferred_element_type=f32
    )
    gated = []
    for k in range(pair_count):
        lanes = slice(k * LANES, (k + 1) * LANES)
        ssd_out = inner[:, lanes] + expand(grown, k) * carried_in[:, lanes]
        gated.append(ssd_out * gating[k])
    squares = gated[0] * gated[0]
    for g in gated[1:]:
        squares = squares + g * g
    inverse = lax.rsqrt(jnp.sum(squares, axis=1, keepdims=True) / width + 1e-05)
    for k in range(pair_count):
        lanes = slice(k * LANES, (k + 1) * LANES)
        mixed[:, lanes] = (gated[k] * inverse * norm_gain_ref[:, lanes]).astype(bf16)

    def out_columns(q):
        return dot(mixed[...], out_w[:, pl.ds(pl.multiple_of(q * cols, cols), cols)])

    away = (2, 1, 3)
    for r in (*away, 0):
        chip = lax.rem(me_x + r, chips)
        mix_out[r] = out_columns(chip * CORES + 1 - core).astype(bf16)
        to_exp(mix_out.at[r], mix_in.at[r], exp_send.at[0], pair_recv.at[r], sibling).start()

    def pair_columns(r):
        value = out_columns(at_chip(r))
        wait_bytes(mix_in, 1, pair_recv.at[r])
        return value + mix_in[r].astype(f32)

    for r in away:
        mix_out[chips + r] = pair_columns(r).astype(bf16)
        to_exp(
            mix_out.at[chips + r],
            mix_in.at[2 * chips - r],
            exp_send.at[1],
            exp_recv.at[0],
            at_chip(r),
        ).start()
    own = pair_columns(0) + stream_ref[...].astype(f32)
    wait_bytes(mix_in, chips - 1, exp_recv.at[0])
    for r in away:
        own = own + mix_in[chips + r].astype(f32)

    hidden[me_e] = own.astype(bf16)
    mine = hidden.at[me_e]
    for r in away:
        to_exp(mine, mine, exp_send.at[3], hidden_recv.at[chips - r], at_chip(r)).start()
    to_exp(mine, mine, exp_send.at[3], hidden_recv.at[0], sibling).start()
    for r in (1, 3, 2):
        wait_bytes(hidden, 1, hidden_recv.at[r])
        block = hidden.at[at_chip(r)]
        to_exp(block, block, exp_send.at[4], hidden_recv.at[chips], sibling).start()
    wait_bytes(hidden, 1, hidden_recv.at[0])
    wait_bytes(hidden, chips - 1, hidden_recv.at[chips])

    tiles = [slice(i * LANES, (i + 1) * LANES) for i in range(cols // LANES)]
    per_part = n_exp // PARTS
    packet = per_dev * per_part

    def places(s, q_in_part):
        return pl.ds(s * per_part + q_in_part, n_ctx, stride=packet)

    def spread_rows(p, q_in_part, value):
        for s in range(per_dev):
            for i, lanes in enumerate(tiles):
                rows_f32.at[p * len(tiles) + i][places(s, q_in_part), :] = value[
                    s * n_ctx : (s + 1) * n_ctx, lanes
                ]

    def pack(ref, p):
        for i, lanes in enumerate(tiles):
            value = rows_f32[p * len(tiles) + i].reshape(n_ctx, packet, LANES)
            ref[p, :, :, lanes] = value.astype(bf16)

    def unpack(ref, p):
        for i, lanes in enumerate(tiles):
            value = ref[p, :, :, lanes].astype(f32)
            rows_f32[p * len(tiles) + i] = value.reshape(n_ctx * packet, LANES)

    def column_rows(s, p, q_in_part):
        return jnp.concatenate(
            [
                rows_f32.at[p * len(tiles) + i][places(s, q_in_part), :]
                for i in range(len(tiles))
            ],
            axis=1,
        ).astype(bf16)

    def exchange_part(src, dst, p, phase):
        exchange(src.at[p], dst.at[p], phase + p)
        dst[p, me_c] = src[p, me_c]

    send_own(2)
    pass_on_neighbours(1)
    pass_on_opposite(0)
    squares = jnp.zeros((token_count, cols), f32)
    for q in range(n_exp):
        h = hidden[q].astype(f32)
        squares = squares + h * h
    inverse = lax.rsqrt(jnp.sum(squares, axis=1, keepdims=True) / d_model + 1e-06)
    for q in range(n_exp):
        columns = slice(q * cols, (q + 1) * cols)
        value = hidden[q].astype(f32) * inverse * moe_gain_ref[:, columns]
        expert_in[:, columns] = value.astype(bf16)
        p, q_in_part = q // per_part, q % per_part
        spread_rows(p, q_in_part, dot(rows_of, expert_in[:, columns]))
        if q_in_part == per_part - 1:
            pack(rows_out, p)
            exchange_part(rows_out, rows_in, p, 2)

    logits = lax.dot_general(expert_in[...], router_ref[...], NT, preferred_element_type=f32)
    named_t, chosen_t = named.T, chosen.T
    score = 1.0 / (1.0 + jnp.exp(-logits))
    picked_score = score * named_t[:, 0:n_ctx]
    gate = picked_score / jnp.sum(picked_score, axis=1, keepdims=True)
    gate_rows = jnp.concatenate([gate] * per_dev, axis=1) * chosen_t
    gate_lead = leading(gate_rows)
    gate_high = gate_lead.astype(bf16)
    gate_low = (gate_rows - gate_lead).astype(bf16)
    pass_on_neighbours(2)
    pass_on_opposite(1)


    for p in range(PARTS):
        wait_bytes(rows_in.at[p], n_ctx - 1, ctx_recv.at[2 + p])
        unpack(rows_in, p)
        for q_in_part in range(per_part):
            first = (p * per_part + q_in_part) * cols
            for s in range(per_dev):
                tokens[s * n_ctx : (s + 1) * n_ctx, first : first + cols] = column_rows(
                    s, p, q_in_part
                )

    complete(0)
    complete(1)

    def hidden_units(first, count):
        units = pl.ds(first, count)
        g = lax.dot_general(tokens[...], w_gate[units, :], NT, preferred_element_type=f32)
        u = lax.dot_general(tokens[...], w_up[units, :], NT, preferred_element_type=f32)
        act[:, units] = (silu(g) * u).astype(bf16)

    chunk = min(256, ff_total)

    def units_step(i, carry):
        hidden_units(pl.multiple_of(i * chunk, chunk), chunk)
        return carry

    early = ff_total // chunk * 3 // 5
    lax.fori_loop(0, early, units_step, 0)
    pass_on_opposite(2)
    lax.fori_loop(early, ff_total // chunk, units_step, 0)
    if ff_total % chunk:
        hidden_units(ff_total // chunk * chunk, ff_total % chunk)

    complete(2)

    for p in range(PARTS):

        def down_step(q_in_part, carry, p=p):
            first = (p * per_part + q_in_part) * cols
            columns = pl.ds(pl.multiple_of(first, cols), cols)
            spread_rows(p, q_in_part, dot(act[...], w_down[:, columns]))
            return carry

        lax.fori_loop(0, per_part, down_step, 0)
        pack(back_out, p)
        exchange_part(back_out, back_in, p, 4)

    def moe_columns(p, q_in_part):
        value = jnp.concatenate([column_rows(s, p, q_in_part) for s in range(per_dev)], axis=0)
        return dot(gate_high, value) + dot(gate_low, value)

    own_part, own_q = me_e // per_part, lax.rem(me_e, per_part)
    for p in range(PARTS):
        wait_bytes(back_in.at[p], n_ctx - 1, ctx_recv.at[4 + p])
        unpack(back_in, p)
        for away in range(per_part - 1, -1, -1):
            q_in_part = lax.rem(own_q + away, per_part)
            q = p * per_part + q_in_part

            def send_columns(q=q, p=p, q_in_part=q_in_part):
                moe_out[q] = moe_columns(p, q_in_part).astype(bf16)
                to_exp(moe_out.at[q], moe_in.at[me_e], exp_send.at[2], exp_recv.at[2], q).start()

            if away:
                send_columns()
            else:
                pl.when(own_part != p)(send_columns)
    total = moe_columns(own_part, own_q) + hidden[me_e].astype(f32)
    wait_bytes(moe_in, n_exp - 1, exp_recv.at[2])
    for d in range(1, n_exp):
        total = total + moe_in[exp_peer(d)].astype(f32)
    out_ref[...] = total.astype(bf16)

    wait_bytes(state_out, n_ctx - 1, ctx_send.at[0])
    wait_bytes(enter_out, n_ctx - 1, ctx_send.at[1])
    wait_bytes(decay_in, n_ctx - 1, ctx_send.at[6])
    for p in range(PARTS):
        wait_bytes(rows_out.at[p], n_ctx - 1, ctx_send.at[2 + p])
        wait_bytes(back_out.at[p], n_ctx - 1, ctx_send.at[4 + p])
    for phase, count in enumerate((chips, chips - 1, n_exp - 1, chips, chips - 1)):
        wait_bytes(mix_out, count, exp_send.at[phase])
    for i in range(3):
        for group, slots in enumerate((2, 1, 1, 2, 1)):
            wait_bytes(w_gate, slots * ff_part, w_send.at[i, group])


def per_device(n_ctx, n_exp, *args):
    (x, z, b, c, step, rate, norm_gain, out_w, stream, moe_gain, router, ids, wg, wu, wd) = args
    t, width = x.shape
    cols = stream.shape[1]
    d_model = cols * n_exp
    ff_part = wg.shape[1]
    ff_total = ff_part * n_exp
    part_rows = width // n_ctx
    stride = SLOTS // n_exp * n_exp
    row_count = n_ctx * (SLOTS // n_exp)
    vmem, dma = pltpu.VMEM, pltpu.SemaphoreType.DMA
    anywhere = pl.BlockSpec(memory_space=pl.ANY)
    rate, norm_gain, moe_gain = (v.reshape(1, -1) for v in (rate, norm_gain, moe_gain))
    router, ids = router.T, ids.T
    inputs = (x, z, b, c, step, rate, norm_gain, out_w, stream, moe_gain, router, ids)
    return pl.pallas_call(
        functools.partial(layer_kernel, n_ctx, n_exp),
        out_shape=jax.ShapeDtypeStruct((t, cols), bf16),
        in_specs=[anywhere] * 15,
        out_specs=pl.BlockSpec(memory_space=pltpu.VMEM),
        scratch_shapes=[
            *(vmem(v.shape, v.dtype) for v in inputs),
            vmem((ff_total, d_model), bf16),
            vmem((ff_total, d_model), bf16),
            vmem((ff_total, d_model), bf16),
            vmem((n_ctx, 2 * part_rows, N), bf16),
            vmem((n_ctx, 2 * part_rows, N), bf16),
            vmem((step.shape[0], 1, N), f32),
            vmem((n_ctx, 1, N), f32),
            vmem((n_ctx, part_rows, N), f32),
            vmem((n_ctx, part_rows, N), f32),
            vmem((t, width), f32),
            vmem((t, width), bf16),
            vmem((n_exp, t, cols), bf16),
            vmem((n_exp, t, cols), bf16),
            vmem((n_exp, t, cols), bf16),
            vmem((t, d_model), bf16),
            vmem((PARTS * cols // LANES, n_ctx * stride // PARTS, LANES), f32),
            vmem((PARTS, n_ctx, stride // PARTS, cols), bf16),
            vmem((PARTS, n_ctx, stride // PARTS, cols), bf16),
            vmem((row_count, d_model), bf16),
            vmem((row_count, ff_total), bf16),
            vmem((PARTS, n_ctx, stride // PARTS, cols), bf16),
            vmem((PARTS, n_ctx, stride // PARTS, cols), bf16),
            vmem((n_exp, t, cols), bf16),
            vmem((n_exp, t, cols), bf16),
            dma((15,)),
            dma((7,)),
            dma((7,)),
            dma((5,)),
            dma((3,)),
            dma((4,)),
            dma((5,)),
            dma((3, 5)),
            dma((3, 6)),
        ],
        compiler_params=pltpu.CompilerParams(
            collective_id=0, has_side_effects=True, vmem_limit_bytes=56 * 1024 * 1024
        ),
        name="layer",
    )(
        *inputs,
        wg[0],
        wu[0],
        wd[0],
    )


def solution(mesh):
    in_specs = (
        P("ctx", "exp"),
        P("ctx", "exp"),
        P("ctx", "exp"),
        P("ctx", "exp"),
        P("exp", "ctx"),
        P("exp"),
        P("exp"),
        P("exp", None),
        P("ctx", "exp"),
        P(),
        P(),
        P("ctx", None),
        P("ctx", "exp", None),
        P("ctx", "exp", None),
        P("ctx", "exp", None),
    )
    return jax.shard_map(
        functools.partial(per_device, mesh.shape["ctx"], mesh.shape["exp"]),
        mesh=mesh,
        in_specs=in_specs,
        out_specs=P("ctx", "exp"),
        check_vma=False,
    )
```
